32 devices in a mesh: rx: 16 (over z, y, core), tm: 2 (over x).
Axes of the slice: x: 2, y: 2, z: 4, core: 2. Of those that a mesh axis runs over, the one named last changes fastest.
Arguments:
- signals: float32 [2, 16, 131072], P(None, 'rx', 'tm'), may hold values from -6 to 6
Outputs:
- ambiguity: float32 [256, 2, 16, 4, 1, 256], P('tm', None, 'rx')
The draws below stay inside these ranges and needn't reach their ends.
All inputs are finite; a program needn't handle non-finite values.
Results may differ from the reference program's by a relative error of at most 0.0003.
Values sent between devices are 32-bit elements; how exact they have to be, the bound alone decides.
No kernel may reach another device: no remote copies, remote signals or barrier semaphores. Data moves between devices by JAX's collectives and lax.ppermute only.
A program may use at most 64 MiB of HBM per device.

```python
import math
import jax
import jax.numpy as jnp
from jax import lax

SEG_LEN = 4096
LAGS = 256
DOPLEN = 512
DOPK = 256
OFFS = 4
REC_DEV = 1
REC = 16
SEGS = 32
SAMPLES = 131072
N_RX = 16


def level_of(rng, extent, pieces, smallest, top_value):
    loudness, own = 1.0, jax.random.fold_in(rng, 6)
    for position, parts in pieces:
        steps = jnp.exp(jax.random.uniform(jax.random.fold_in(own, position), (parts,), jnp.float32, smallest / len(pieces), top_value / len(pieces)))
        loudness = loudness * jnp.repeat(steps, extent[position] // parts).reshape([-1 if axis == position else 1 for axis in range(len(extent))])
    return loudness


def gaussian(own_key, extent, deviation, limit, pieces=(), kind=jnp.bfloat16):
    values = jax.random.normal(own_key, extent, jnp.float32) * deviation
    if len(pieces) > 0:
        values = level_of(own_key, extent, pieces, -0.22, 0.18) * values
    return jnp.clip(values, min=-limit, max=limit).astype(kind)


def setup_inputs(seed: int = 0) -> dict:
    arg_keys = jax.random.split(jax.random.key(seed), 2)
    return {
        "signals": gaussian(arg_keys[0], (2, REC, SAMPLES), 1.0, 6.0, ((1, 16), (2, 2)), jnp.float32),
    }


def reference(signals):
    field = lax.complex(signals[0], signals[1])
    segments = field.reshape(REC, SEGS, SEG_LEN)
    spectra = jnp.fft.fft(segments, axis=-1)
    half = LAGS // 2
    seg_index = jnp.arange(SEGS, dtype=jnp.int32)
    freq_index = jnp.arange(DOPK, dtype=jnp.int32) - DOPK // 2
    phase = (seg_index[:, None] * freq_index[None, :] % DOPLEN).astype(jnp.float32)
    angle = 2.0 * math.pi / DOPLEN * phase
    dop_cos = jnp.cos(angle)
    dop_sin = -jnp.sin(angle)
    highest = lax.Precision.HIGHEST

    def one_group(group):
        own = lax.dynamic_slice_in_dim(spectra, (group * REC_DEV).astype(jnp.int32), REC_DEV, 0)
        blocks = []
        for step in range(1, OFFS + 1):
            far_group = ((group - step) % N_RX).astype(jnp.int32)
            far = lax.dynamic_slice_in_dim(spectra, far_group * REC_DEV, REC_DEV, 0)
            product = own[:, None] * jnp.conj(far[None])
            full = jnp.fft.ifft(product, axis=-1)
            kept = jnp.concatenate([full[..., SEG_LEN - half:], full[..., :half]], axis=-1)
            corr_re = jnp.real(kept)
            corr_im = jnp.imag(kept)
            amb_re = jnp.einsum('absl,sf->labf', corr_re, dop_cos, precision=highest) - jnp.einsum('absl,sf->labf', corr_im, dop_sin, precision=highest)
            amb_im = jnp.einsum('absl,sf->labf', corr_re, dop_sin, precision=highest) + jnp.einsum('absl,sf->labf', corr_im, dop_cos, precision=highest)
            blocks.append(jnp.stack([amb_re, amb_im], axis=1))
        return jnp.stack(blocks, axis=3)
    groups = lax.map(one_group, jnp.arange(N_RX, dtype=jnp.int32))
    scale = 1.0 / math.sqrt(2.0 * SEG_LEN * SEGS)
    result = jnp.moveaxis(groups, 0, 2).reshape(LAGS, 2, REC, OFFS, REC_DEV, DOPK) * scale
    return result.astype(jnp.float32)
```

```python
import functools
import math

import jax
import jax.numpy as jnp
from jax import lax
from jax.experimental import pallas as pl
from jax.experimental.pallas import tpu as pltpu
from jax.sharding import PartitionSpec as P

SEG_LEN = 4096
LAGS = 256
DOPLEN = 512
DOPK = 256
OFFS = 4

HALF = LAGS // 2
BLOCK = LAGS
WINDOW = 2 * LAGS
BLOCKS = SEG_LEN // BLOCK
ROWS = SEG_LEN // HALF

VMEM = pl.BlockSpec(memory_space=pltpu.VMEM)
SMEM = pl.BlockSpec(memory_space=pltpu.SMEM)


def trig(rows, columns, first_row, first_column):
    fine = 16
    coarse = rows // fine
    column = jnp.arange(columns, dtype=jnp.int32)[None, :] + first_column
    unit = 2.0 * math.pi / WINDOW
    big_row = fine * jnp.arange(coarse, dtype=jnp.int32)[:, None] + first_row
    big = unit * (big_row * column % WINDOW).astype(jnp.float32)
    small_row = jnp.arange(fine, dtype=jnp.int32)[:, None]
    small = unit * (small_row * column % WINDOW).astype(jnp.float32)
    cb, sb, cs, ss = lax.optimization_barrier(
        (jnp.cos(big), jnp.sin(big), jnp.cos(small), jnp.sin(small))
    )
    cb, sb, cs, ss = (cb[:, None], sb[:, None], cs[None], ss[None])
    cos = (cb * cs - sb * ss).reshape(rows, columns)
    sin = (sb * cs + cb * ss).reshape(rows, columns)
    return cos, sin


def split(value):
    high = value.astype(jnp.bfloat16)
    low = (value - high.astype(jnp.float32)).astype(jnp.bfloat16)
    return high, low


def split_table(value):
    high = lax.reduce_precision(value, exponent_bits=8, mantissa_bits=7)
    return high.astype(jnp.bfloat16), (value - high).astype(jnp.bfloat16)


def product(left, table_high, table_low):
    high, low = split(left)
    count = left.shape[0]
    both = jnp.dot(
        jnp.concatenate([high, low], axis=0), table_high, preferred_element_type=jnp.float32
    )
    rest = jnp.dot(high, table_low, preferred_element_type=jnp.float32)
    return both[:count] + both[count:] + rest


def gather_rows(piece_ref, scratch, column, plane, first, segs):
    for block in range(BLOCKS):
        half = (2 * block + first) % ROWS
        scratch[pl.ds(block * segs, segs), pl.ds(column, HALF)] = piece_ref[
            plane, pl.ds(half, segs, stride=ROWS), :
        ]


def transform(piece_ref, scratch, table_high, table_low, firsts, segs):
    rows = BLOCKS * segs
    for plane in range(2):
        for place, first in enumerate(firsts):
            gather_rows(piece_ref, scratch, plane * BLOCK + place * HALF, plane, first, segs)
    straight = scratch[...]
    crossed = jnp.concatenate([straight[:, BLOCK:], -straight[:, :BLOCK]], axis=1)
    out = product(jnp.concatenate([straight, crossed], axis=0), table_high[...], table_low[...])
    return out[:rows], out[rows:]


def own_kernel(segs, *refs):
    pieces = refs[:OFFS]
    y_high, y_low, x_high, x_low, x_out, y_out, _, scratch = refs[OFFS:]
    for slot, piece in enumerate(pieces):
        y_re, y_im = transform(piece, scratch, y_high, y_low, (1, 2), segs)
        y_out[slot, :, :WINDOW] = y_re
        y_out[slot, :, WINDOW:] = y_im
        x_re, x_im = transform(piece, scratch, x_high, x_low, (0, 3), segs)
        x_out[slot, :, :WINDOW] = y_re + x_re
        x_out[slot, :, WINDOW:] = y_im + x_im


def far_kernel(segs, piece, y_high, y_low, _, y_out, scratch):
    y_re, y_im = transform(piece, scratch, y_high, y_low, (1, 2), segs)
    y_out[0, :, :WINDOW] = y_re
    y_out[0, :, WINDOW:] = y_im


def swap_halves(value):
    return pltpu.roll(value, value.shape[0] // 2, axis=0)


def pair_kernel(
    segs, parts, place, x_ref, own_ref, far_ref, t_high, t_low, keep_ref, send_ref, spectrum, held
):
    me, my_part = place[0], place[1]
    tile = 2 * segs
    lag_dev = LAGS // parts
    first_half = lax.broadcasted_iota(jnp.int32, (tile, HALF), 0) < segs
    for q in range(OFFS):
        x_slot = q ^ me
        for column in range(0, WINDOW, HALF):
            re = [jnp.zeros((tile, HALF), jnp.float32) for _ in range(OFFS)]
            im = [jnp.zeros((tile, HALF), jnp.float32) for _ in range(OFFS)]
            for row in range(0, BLOCKS * segs, tile):
                rows = pl.ds(row, tile)
                x_re = x_ref[x_slot, rows, pl.ds(column, HALF)]
                x_im = x_ref[x_slot, rows, pl.ds(WINDOW + column, HALF)]
                for o in range(OFFS):
                    p = q - 1 - o
                    y_ref = own_ref if p >= 0 else far_ref
                    y_slot = (p % OFFS) ^ me
                    y_re = y_ref[y_slot, rows, pl.ds(column, HALF)]
                    y_im = y_ref[y_slot, rows, pl.ds(WINDOW + column, HALF)]
                    re[o] = re[o] + (x_re * y_re + x_im * y_im)
                    im[o] = im[o] + (x_im * y_re - x_re * y_im)
            for o in range(0, OFFS, 2):
                for values, base in ((re, 0), (im, WINDOW)):
                    a, b = values[o], values[o + 1]
                    folded = jnp.where(first_half, a, b) + swap_halves(
                        jnp.where(first_half, b, a)
                    )
                    spectrum[
                        pl.ds((q * OFFS + o) * segs, tile), pl.ds(base + column, HALF)
                    ] = folded
    s_re, s_im = spectrum[:, :WINDOW], spectrum[:, WINDOW:]
    left = jnp.concatenate(
        [jnp.concatenate([s_re, -s_im], axis=1), jnp.concatenate([s_im, s_re], axis=1)], axis=0
    )
    corr = product(left, t_high[...], t_low[...])
    count = OFFS * OFFS * segs
    wide_half = lax.broadcasted_iota(jnp.int32, (tile, LAGS), 0) < segs
    for q in range(OFFS):
        for o in range(0, OFFS, 2):
            row = (q * OFFS + o) * segs
            re = corr[row : row + tile]
            im = corr[count + row : count + row + tile]
            first = jnp.where(wide_half, re, swap_halves(im))
            second = jnp.where(wide_half, swap_halves(re), im)
            for t in range(parts):
                lanes = slice(t * lag_dev, (t + 1) * lag_dev)
                held[t * OFFS + q, pl.ds(o * tile, tile), :] = first[:, lanes]
                held[t * OFFS + q, pl.ds((o + 1) * tile, tile), :] = second[:, lanes]
    for dy in range(2):
        for dt in range(parts):
            there = lax.rem(my_part + dt, parts) * OFFS
            q = me ^ (2 * dy)
            keep_ref[dy, dt] = held[there + q]
            send_ref[dy, dt] = held[there + (q ^ 1)]


def doppler_kernel(segs, keep_ref, recv_ref, *refs):
    others, (table, out_ref) = refs[:-2], refs[-2:]
    tile = 2 * segs
    lag_dev = out_ref.shape[0] // (2 * OFFS * DOPK // HALF)
    stride = out_ref.shape[0] // lag_dev
    per = DOPK // HALF
    for o in range(OFFS):
        rows = pl.ds(o * tile, tile)
        tiles = [keep_ref[0, 0, rows, :], recv_ref[0, 0, rows, :]]
        for other in others:
            tiles += [other[0, rows, :], other[1, rows, :]]
        high, low = split(jnp.concatenate(tiles, axis=0))
        left = jnp.concatenate([high, low, high], axis=0)
        out = lax.dot_general(
            left, table[...], (((0,), (0,)), ((), ())), preferred_element_type=jnp.float32
        )
        for c in range(2):
            for f in range(per):
                where = (c * OFFS + o) * per + f
                first = c * DOPK + f * HALF
                out_ref[pl.ds(where, lag_dev, stride=stride), :] = out[:, first : first + HALF]


def doppler_table(sources, seg_dev, segs, scale):
    segment = jnp.concatenate(
        [part * seg_dev + slot * segs + jnp.arange(segs, dtype=jnp.int32) for slot, part in sources]
    )
    frequency = jnp.arange(DOPK, dtype=jnp.int32) - DOPK // 2
    angle = (
        2.0 * math.pi / DOPLEN
        * (segment[:, None] * frequency[None, :] % DOPLEN).astype(jnp.float32)
    )
    cos, sin = (jnp.cos(angle) * scale, jnp.sin(angle) * scale)
    cos = cos.reshape(len(sources), 1, segs, DOPK)
    sin = sin.reshape(len(sources), 1, segs, DOPK)
    table = jnp.concatenate(
        [jnp.concatenate([cos, -sin], axis=3), jnp.concatenate([sin, cos], axis=3)], axis=1
    ).reshape(2 * len(sources) * segs, 2 * DOPK)
    high, low = split_table(table)
    return jnp.concatenate([high, high, low], axis=0)


def per_device(count, parts, signals):
    rec_dev, length = signals.shape[1], signals.shape[2]
    seg_dev = length // SEG_LEN
    segs = seg_dev // OFFS
    assert rec_dev == 1 and count % OFFS == 0 and seg_dev % OFFS == 0
    me = lax.axis_index("rx") % OFFS
    my_part = lax.axis_index("tm")
    place = jnp.stack([me, my_part]).astype(jnp.int32)

    def move(value, flip, ahead=0, later=0):
        pairs = []
        for r in range(count):
            for t in range(parts):
                to = ((r ^ flip) + ahead) % count
                pairs.append((r * parts + t, to * parts + (t + later) % parts))
        return lax.ppermute(value, ("rx", "tm"), pairs)

    raw = signals.reshape(2, seg_dev * ROWS, HALF)
    own, far = [], []
    for slot in range(OFFS):
        piece = lax.dynamic_slice_in_dim(raw, (me ^ slot) * (segs * ROWS), segs * ROWS, axis=1)
        own.append(move(piece, slot) if slot else piece)
    for slot in range(OFFS):
        far.append(move(own[slot], 0, ahead=OFFS))

    cos, sin = trig(WINDOW, WINDOW, -HALF, 0)
    near = slice(HALF, HALF + BLOCK)
    y_high, y_low = split_table(jnp.concatenate([cos[near], sin[near]], axis=0))
    x_high, x_low = split_table(
        jnp.concatenate([cos[:HALF], cos[HALF + BLOCK :], sin[:HALF], sin[HALF + BLOCK :]], axis=0)
    )
    cos, sin = trig(WINDOW, LAGS, 0, -HALF)
    t_high, t_low = split_table(jnp.concatenate([cos, sin], axis=0) / WINDOW)

    rows = BLOCKS * segs
    spectra = jax.ShapeDtypeStruct((OFFS, rows, 2 * WINDOW), jnp.float32)
    scratch = pltpu.VMEM((rows, 2 * BLOCK), jnp.float32)
    x_own, y_own, y_far = pl.pallas_call(
        functools.partial(own_kernel, segs),
        out_shape=(spectra, spectra, spectra),
        in_specs=[VMEM] * (OFFS + 4),
        out_specs=(VMEM, VMEM, pl.BlockSpec(memory_space=pl.ANY)),
        scratch_shapes=[scratch],
        name="own",
    )(*own, y_high, y_low, x_high, x_low)
    for slot in range(OFFS):
        y_far = pl.pallas_call(
            functools.partial(far_kernel, segs),
            grid=(1,),
            out_shape=spectra,
            in_specs=[VMEM, VMEM, VMEM, pl.BlockSpec(memory_space=pl.ANY)],
            out_specs=pl.BlockSpec((1, rows, 2 * WINDOW), lambda i, slot=slot: (slot, 0, 0)),
            scratch_shapes=[scratch],
            input_output_aliases={3: 0},
            name="far",
        )(far[slot], y_high, y_low, y_far)

    lag_dev = LAGS // parts
    piece_rows = OFFS * 2 * segs
    pieces = jax.ShapeDtypeStruct((2, parts, piece_rows, lag_dev), jnp.float32)
    keep, send = pl.pallas_call(
        functools.partial(pair_kernel, segs, parts),
        out_shape=(pieces, pieces),
        in_specs=[SMEM] + [VMEM] * 5,
        out_specs=(VMEM, VMEM),
        scratch_shapes=[
            pltpu.VMEM((OFFS * OFFS * segs, 2 * WINDOW), jnp.float32),
            pltpu.VMEM((parts * OFFS, piece_rows, lag_dev), jnp.float32),
        ],
        name="pair",
    )(place, x_own, y_own, y_far, t_high, t_low)

    recv = move(send, 1)
    others = []
    sources = [(me, my_part), (me ^ 1, my_part)]
    for dy in range(2):
        for dt in range(parts):
            if dy or dt:
                others.append(move(jnp.stack([keep[dy, dt], recv[dy, dt]]), 2 * dy, later=dt))
                slot, part = me ^ (2 * dy), (my_part - dt) % parts
                sources += [(slot, part), (slot ^ 1, part)]

    scale = 1.0 / math.sqrt(2.0 * SEG_LEN * seg_dev * parts)
    table = doppler_table(sources, seg_dev, segs, scale)
    out_rows = lag_dev * 2 * OFFS * DOPK // HALF
    out = pl.pallas_call(
        functools.partial(doppler_kernel, segs),
        out_shape=jax.ShapeDtypeStruct((out_rows, HALF), jnp.float32),
        in_specs=[VMEM] * (len(others) + 3),
        out_specs=VMEM,
        name="doppler",
    )(keep, recv, *others, table)
    return out.reshape(lag_dev, 2, 1, OFFS, 1, DOPK)


def solution(mesh):
    count, parts = mesh.shape["rx"], mesh.shape["tm"]
    return jax.shard_map(
        functools.partial(per_device, count, parts),
        mesh=mesh,
        in_specs=(P(None, "rx", "tm"),),
        out_specs=P("tm", None, "rx", None, None, None),
        check_vma=False,
    )
```

```python
import functools
import math

import jax
import jax.numpy as jnp
from jax import lax
from jax.experimental import pallas as pl
from jax.experimental.pallas import tpu as pltpu
from jax.sharding import PartitionSpec as P

SEG_LEN = 4096
LAGS = 256
DOPLEN = 512
DOPK = 256
OFFS = 4

HALF = LAGS // 2
BLOCK = LAGS
WINDOW = 2 * LAGS
BLOCKS = SEG_LEN // BLOCK
ROWS = SEG_LEN // HALF

VMEM = pl.BlockSpec(memory_space=pltpu.VMEM)
SMEM = pl.BlockSpec(memory_space=pltpu.SMEM)

def limit(mib):
    return pltpu.CompilerParams(vmem_limit_bytes=mib << 20)


def trig(rows, columns, first_row, first_column):
    fine = 16
    coarse = rows // fine
    column = jnp.arange(columns, dtype=jnp.int32)[None, :] + first_column
    unit = 2.0 * math.pi / WINDOW
    big_row = fine * jnp.arange(coarse, dtype=jnp.int32)[:, None] + first_row
    big = unit * (big_row * column % WINDOW).astype(jnp.float32)
    small_row = jnp.arange(fine, dtype=jnp.int32)[:, None]
    small = unit * (small_row * column % WINDOW).astype(jnp.float32)
    cb, sb, cs, ss = lax.optimization_barrier(
        (jnp.cos(big), jnp.sin(big), jnp.cos(small), jnp.sin(small))
    )
    cb, sb, cs, ss = (cb[:, None], sb[:, None], cs[None], ss[None])
    cos = (cb * cs - sb * ss).reshape(rows, columns)
    sin = (sb * cs + cb * ss).reshape(rows, columns)
    return cos, sin


def split(value):
    high = value.astype(jnp.bfloat16)
    low = (value - high.astype(jnp.float32)).astype(jnp.bfloat16)
    return high, low


def split_table(value):
    high = lax.reduce_precision(value, exponent_bits=8, mantissa_bits=7)
    return high.astype(jnp.bfloat16), (value - high).astype(jnp.bfloat16)


def product(left, table_high, table_low):
    high, low = split(left)
    count = left.shape[0]
    both = jnp.dot(
        jnp.concatenate([high, low], axis=0), table_high, preferred_element_type=jnp.float32
    )
    rest = jnp.dot(high, table_low, preferred_element_type=jnp.float32)
    return both[:count] + both[count:] + rest


def gather_rows(piece_ref, scratch, column, plane, first, segs):
    for block in range(BLOCKS):
        half = (2 * block + first) % ROWS
        scratch[pl.ds(block * segs, segs), pl.ds(column, HALF)] = piece_ref[
            plane, pl.ds(half, segs, stride=ROWS), :
        ]


def transform(piece_ref, scratch, table_high, table_low, firsts, segs):
    rows = BLOCKS * segs
    for plane in range(2):
        for place, first in enumerate(firsts):
            gather_rows(piece_ref, scratch, plane * BLOCK + place * HALF, plane, first, segs)
    straight = scratch[...]
    crossed = jnp.concatenate([straight[:, BLOCK:], -straight[:, :BLOCK]], axis=1)
    out = product(jnp.concatenate([straight, crossed], axis=0), table_high[...], table_low[...])
    return out[:rows], out[rows:]


def own_kernel(segs, *refs):
    pieces = refs[:OFFS]
    y_high, y_low, x_high, x_low, x_out, y_out, _, scratch = refs[OFFS:]
    for slot, piece in enumerate(pieces):
        y_re, y_im = transform(piece, scratch, y_high, y_low, (1, 2), segs)
        y_out[slot, :, :WINDOW] = y_re
        y_out[slot, :, WINDOW:] = y_im
        x_re, x_im = transform(piece, scratch, x_high, x_low, (0, 3), segs)
        x_out[slot, :, :WINDOW] = y_re + x_re
        x_out[slot, :, WINDOW:] = y_im + x_im


def far_kernel(segs, piece, y_high, y_low, _, y_out, scratch):
    y_re, y_im = transform(piece, scratch, y_high, y_low, (1, 2), segs)
    y_out[0, :, :WINDOW] = y_re
    y_out[0, :, WINDOW:] = y_im


def swap_halves(value):
    return pltpu.roll(value, value.shape[0] // 2, axis=0)


def pair_kernel(
    segs, parts, place, x_ref, own_ref, far_ref, t_high, t_low, keep_ref, send_ref, spectrum, held
):
    me, my_part = place[0], place[1]
    tile = 2 * segs
    lag_dev = LAGS // parts
    first_half = lax.broadcasted_iota(jnp.int32, (tile, HALF), 0) < segs
    for q in range(OFFS):
        x_slot = q ^ me
        for column in range(0, WINDOW, HALF):
            re = [jnp.zeros((tile, HALF), jnp.float32) for _ in range(OFFS)]
            im = [jnp.zeros((tile, HALF), jnp.float32) for _ in range(OFFS)]
            for row in range(0, BLOCKS * segs, tile):
                rows = pl.ds(row, tile)
                x_re = x_ref[x_slot, rows, pl.ds(column, HALF)]
                x_im = x_ref[x_slot, rows, pl.ds(WINDOW + column, HALF)]
                for o in range(OFFS):
                    p = q - 1 - o
                    y_ref = own_ref if p >= 0 else far_ref
                    y_slot = (p % OFFS) ^ me
                    y_re = y_ref[y_slot, rows, pl.ds(column, HALF)]
                    y_im = y_ref[y_slot, rows, pl.ds(WINDOW + column, HALF)]
                    re[o] = re[o] + (x_re * y_re + x_im * y_im)
                    im[o] = im[o] + (x_im * y_re - x_re * y_im)
            for o in range(0, OFFS, 2):
                for values, base in ((re, 0), (im, WINDOW)):
                    a, b = values[o], values[o + 1]
                    folded = jnp.where(first_half, a, b) + swap_halves(
                        jnp.where(first_half, b, a)
                    )
                    spectrum[
                        pl.ds((q * OFFS + o) * segs, tile), pl.ds(base + column, HALF)
                    ] = folded
    s_re, s_im = spectrum[:, :WINDOW], spectrum[:, WINDOW:]
    left = jnp.concatenate(
        [jnp.concatenate([s_re, -s_im], axis=1), jnp.concatenate([s_im, s_re], axis=1)], axis=0
    )
    corr = product(left, t_high[...], t_low[...])
    count = OFFS * OFFS * segs
    wide_half = lax.broadcasted_iota(jnp.int32, (tile, LAGS), 0) < segs
    for q in range(OFFS):
        for o in range(0, OFFS, 2):
            row = (q * OFFS + o) * segs
            re = corr[row : row + tile]
            im = corr[count + row : count + row + tile]
            first = jnp.where(wide_half, re, swap_halves(im))
            second = jnp.where(wide_half, swap_halves(re), im)
            for t in range(parts):
                lanes = slice(t * lag_dev, (t + 1) * lag_dev)
                held[t * OFFS + q, pl.ds(o * tile, tile), :] = first[:, lanes]
                held[t * OFFS + q, pl.ds((o + 1) * tile, tile), :] = second[:, lanes]
    for dy in range(2):
        for dt in range(parts):
            there = lax.rem(my_part + dt, parts) * OFFS
            q = me ^ (2 * dy)
            keep_ref[dy, dt] = held[there + q]
            send_ref[dy, dt] = held[there + (q ^ 1)]


def doppler_kernel(segs, keep_ref, recv_ref, *refs):
    others, (table, out_ref) = refs[:-2], refs[-2:]
    tile = 2 * segs
    lag_dev = out_ref.shape[0] // (2 * OFFS * DOPK // HALF)
    stride = out_ref.shape[0] // lag_dev
    per = DOPK // HALF
    for o in range(OFFS):
        rows = pl.ds(o * tile, tile)
        tiles = [keep_ref[0, 0, rows, :], recv_ref[0, 0, rows, :]]
        for other in others:
            tiles += [other[0, rows, :], other[1, rows, :]]
        high, low = split(jnp.concatenate(tiles, axis=0))
        left = jnp.concatenate([high, low, high], axis=0)
        out = lax.dot_general(
            left, table[...], (((0,), (0,)), ((), ())), preferred_element_type=jnp.float32
        )
        for c in range(2):
            for f in range(per):
                where = (c * OFFS + o) * per + f
                first = c * DOPK + f * HALF
                out_ref[pl.ds(where, lag_dev, stride=stride), :] = out[:, first : first + HALF]


def doppler_table(sources, seg_dev, segs, scale):
    segment = jnp.concatenate(
        [part * seg_dev + slot * segs + jnp.arange(segs, dtype=jnp.int32) for slot, part in sources]
    )
    frequency = jnp.arange(DOPK, dtype=jnp.int32) - DOPK // 2
    angle = (
        2.0 * math.pi / DOPLEN
        * (segment[:, None] * frequency[None, :] % DOPLEN).astype(jnp.float32)
    )
    cos, sin = (jnp.cos(angle) * scale, jnp.sin(angle) * scale)
    cos = cos.reshape(len(sources), 1, segs, DOPK)
    sin = sin.reshape(len(sources), 1, segs, DOPK)
    table = jnp.concatenate(
        [jnp.concatenate([cos, -sin], axis=3), jnp.concatenate([sin, cos], axis=3)], axis=1
    ).reshape(2 * len(sources) * segs, 2 * DOPK)
    high, low = split_table(table)
    return jnp.concatenate([high, high, low], axis=0)


def per_device(count, parts, signals):
    rec_dev, length = signals.shape[1], signals.shape[2]
    seg_dev = length // SEG_LEN
    segs = seg_dev // OFFS
    assert rec_dev == 1 and count % OFFS == 0 and seg_dev % OFFS == 0
    me = lax.axis_index("rx") % OFFS
    my_part = lax.axis_index("tm")
    place = jnp.stack([me, my_part]).astype(jnp.int32)

    def move(value, flip, ahead=0, later=0):
        pairs = []
        for r in range(count):
            for t in range(parts):
                to = ((r ^ flip) + ahead) % count
                pairs.append((r * parts + t, to * parts + (t + later) % parts))
        return lax.ppermute(value, ("rx", "tm"), pairs)

    raw = signals.reshape(2, seg_dev * ROWS, HALF)
    own, far = [], []
    for slot in range(OFFS):
        piece = lax.dynamic_slice_in_dim(raw, (me ^ slot) * (segs * ROWS), segs * ROWS, axis=1)
        own.append(move(piece, slot) if slot else piece)
    for slot in range(OFFS):
        far.append(move(own[slot], 0, ahead=OFFS))

    cos, sin = trig(WINDOW, WINDOW, -HALF, 0)
    near = slice(HALF, HALF + BLOCK)
    y_high, y_low = split_table(jnp.concatenate([cos[near], sin[near]], axis=0))
    x_high, x_low = split_table(
        jnp.concatenate([cos[:HALF], cos[HALF + BLOCK :], sin[:HALF], sin[HALF + BLOCK :]], axis=0)
    )
    cos, sin = trig(WINDOW, LAGS, 0, -HALF)
    t_high, t_low = split_table(jnp.concatenate([cos, sin], axis=0) / WINDOW)

    rows = BLOCKS * segs
    spectra = jax.ShapeDtypeStruct((OFFS, rows, 2 * WINDOW), jnp.float32)
    scratch = pltpu.VMEM((rows, 2 * BLOCK), jnp.float32)
    x_own, y_own, y_far = pl.pallas_call(
        functools.partial(own_kernel, segs),
        out_shape=(spectra, spectra, spectra),
        in_specs=[VMEM] * (OFFS + 4),
        out_specs=(VMEM, VMEM, pl.BlockSpec(memory_space=pl.ANY)),
        scratch_shapes=[scratch],
        compiler_params=limit(8),
        name="own",
    )(*own, y_high, y_low, x_high, x_low)
    for slot in range(OFFS):
        y_far = pl.pallas_call(
            functools.partial(far_kernel, segs),
            grid=(1,),
            out_shape=spectra,
            in_specs=[VMEM, VMEM, VMEM, pl.BlockSpec(memory_space=pl.ANY)],
            out_specs=pl.BlockSpec((1, rows, 2 * WINDOW), lambda i, slot=slot: (slot, 0, 0)),
            scratch_shapes=[scratch],
            input_output_aliases={3: 0},
            compiler_params=limit(4),
        name="far",
        )(far[slot], y_high, y_low, y_far)

    lag_dev = LAGS // parts
    piece_rows = OFFS * 2 * segs
    pieces = jax.ShapeDtypeStruct((2, parts, piece_rows, lag_dev), jnp.float32)
    keep, send = pl.pallas_call(
        functools.partial(pair_kernel, segs, parts),
        out_shape=(pieces, pieces),
        in_specs=[SMEM] + [VMEM] * 5,
        out_specs=(VMEM, VMEM),
        scratch_shapes=[
            pltpu.VMEM((OFFS * OFFS * segs, 2 * WINDOW), jnp.float32),
            pltpu.VMEM((parts * OFFS, piece_rows, lag_dev), jnp.float32),
        ],
        compiler_params=limit(8),
        name="pair",
    )(place, x_own, y_own, y_far, t_high, t_low)

    recv = move(send, 1)
    others = []
    sources = [(me, my_part), (me ^ 1, my_part)]
    for dy in range(2):
        for dt in range(parts):
            if dy or dt:
                others.append(move(jnp.stack([keep[dy, dt], recv[dy, dt]]), 2 * dy, later=dt))
                slot, part = me ^ (2 * dy), (my_part - dt) % parts
                sources += [(slot, part), (slot ^ 1, part)]

    scale = 1.0 / math.sqrt(2.0 * SEG_LEN * seg_dev * parts)
    table = doppler_table(sources, seg_dev, segs, scale)
    out_rows = lag_dev * 2 * OFFS * DOPK // HALF
    out = pl.pallas_call(
        functools.partial(doppler_kernel, segs),
        out_shape=jax.ShapeDtypeStruct((out_rows, HALF), jnp.float32),
        in_specs=[VMEM] * (len(others) + 3),
        out_specs=VMEM,
        compiler_params=limit(4),
        name="doppler",
    )(keep, recv, *others, table)
    return out.reshape(lag_dev, 2, 1, OFFS, 1, DOPK)


def solution(mesh):
    count, parts = mesh.shape["rx"], mesh.shape["tm"]
    return jax.shard_map(
        functools.partial(per_device, count, parts),
        mesh=mesh,
        in_specs=(P(None, "rx", "tm"),),
        out_specs=P("tm", None, "rx", None, None, None),
        check_vma=False,
    )
```

```python
import functools
import math

import jax
import jax.numpy as jnp
import numpy as np
from jax import lax
from jax.experimental import pallas as pl
from jax.experimental.pallas import tpu as pltpu
from jax.sharding import PartitionSpec as P


SEG_LEN = 4096
LAGS = 256
DOPLEN = 512
DOPK = 256
OFFS = 4

HALF = LAGS // 2
BLOCK = LAGS
WINDOW = 2 * LAGS
BLOCKS = SEG_LEN // BLOCK
ROWS = SEG_LEN // HALF
STORES = 4

VMEM = pl.BlockSpec(memory_space=pltpu.VMEM)
SMEM = pl.BlockSpec(memory_space=pltpu.SMEM)
HBM = pl.BlockSpec(memory_space=pltpu.HBM)
ANY = pl.BlockSpec(memory_space=pl.ANY)


def limit(mib):
    return pltpu.CompilerParams(vmem_limit_bytes=mib << 20)


RELAYED = (0, 2, 3)


def halves(table):
    high = table.astype(jnp.bfloat16)
    return jnp.asarray(high), jnp.asarray((table - high.astype(np.float64)).astype(jnp.bfloat16))


def trig(rows, columns):
    angle = 2.0 * math.pi / WINDOW * (np.outer(rows, columns) % WINDOW)
    return np.concatenate([np.cos(angle), np.sin(angle)], axis=0)


def split(value):
    high = value.astype(jnp.bfloat16)
    low = (value - high.astype(jnp.float32)).astype(jnp.bfloat16)
    return high, low


def split_table(value):
    high = lax.reduce_precision(value, exponent_bits=8, mantissa_bits=7)
    return high.astype(jnp.bfloat16), (value - high).astype(jnp.bfloat16)


def product(left, table_high, table_low):
    high, low = split(left)
    count = left.shape[0]
    both = jnp.dot(
        jnp.concatenate([high, low], axis=0), table_high, preferred_element_type=jnp.float32
    )
    rest = jnp.dot(high, table_low, preferred_element_type=jnp.float32)
    return both[:count] + both[count:] + rest


def gather_rows(piece_ref, scratch, row, firsts, segs):
    for plane in range(2):
        for position, first in enumerate(firsts):
            column = pl.ds(plane * BLOCK + position * HALF, HALF)
            for block in range(BLOCKS):
                half = (2 * block + first) % ROWS
                scratch[pl.ds(row + block * segs, segs), column] = piece_ref[
                    plane, pl.ds(half, segs, stride=ROWS), :
                ]


def transform(scratch, table_high, table_low):
    straight = scratch[...]
    count = straight.shape[0]
    crossed = jnp.concatenate([straight[:, BLOCK:], -straight[:, :BLOCK]], axis=1)
    out = product(jnp.concatenate([straight, crossed], axis=0), table_high[...], table_low[...])
    return out[:count], out[count:]


def swap_halves(value):
    return pltpu.roll(value, value.shape[0] // 2, axis=0)


def pair_sum(x_ref, x_slot, y_ref, y_slot, column, tile):
    re, im = None, None
    for row in range(0, x_ref.shape[1], tile):
        rows = pl.ds(row, tile)
        x_re = x_ref[x_slot, rows, pl.ds(column, HALF)]
        x_im = x_ref[x_slot, rows, pl.ds(WINDOW + column, HALF)]
        y_re = y_ref[y_slot, rows, pl.ds(column, HALF)]
        y_im = y_ref[y_slot, rows, pl.ds(WINDOW + column, HALF)]
        more_re = x_re * y_re + x_im * y_im
        more_im = x_im * y_re - x_re * y_im
        re, im = (more_re, more_im) if re is None else (re + more_re, im + more_im)
    return re, im


def near_pairs(segs, me, x_ref, y_ref, spectrum):
    tile = 2 * segs
    first_half = lax.broadcasted_iota(jnp.int32, (tile, HALF), 0) < segs
    zero = jnp.zeros((tile, HALF), jnp.float32)
    for q in range(OFFS):
        for column in range(0, WINDOW, HALF):
            sums = [
                pair_sum(x_ref, q ^ me, y_ref, (q - 1 - o) ^ me, column, tile)
                if o < q
                else (zero, zero)
                for o in range(OFFS)
            ]
            for o in range(0, OFFS, 2):
                rows = pl.ds((q * OFFS + o) * segs, tile)
                for part, base in ((0, 0), (1, WINDOW)):
                    a, b = sums[o][part], sums[o + 1][part]
                    spectrum[rows, pl.ds(base + column, HALF)] = jnp.where(
                        first_half, a, b
                    ) + swap_halves(jnp.where(first_half, b, a))


def far_pair(segs, q, r, x_ref, x_slot, y_ref, spectrum, first_row):
    tile = 2 * segs
    o = q + (OFFS - 1) - r

    @pl.when(q <= r)
    def _():
        second = lax.broadcasted_iota(jnp.int32, (tile, HALF), 0) >= segs
        mine = second == (lax.rem(o, 2) == 1)
        rows = pl.ds(pl.multiple_of(first_row + (o - lax.rem(o, 2)) * segs, tile), tile)
        for column in range(0, WINDOW, HALF):
            sums = pair_sum(x_ref, x_slot, y_ref, 0, column, tile)
            for value, base in zip(sums, (0, WINDOW)):
                columns = pl.ds(base + column, HALF)
                total = value + swap_halves(value)
                spectrum[rows, columns] = spectrum[rows, columns] + jnp.where(mine, total, 0.0)


def own_transform(piece, slot, table_high, table_low, x_out, y_out, scratch, segs):
    rows = BLOCKS * segs
    odd = lax.broadcasted_iota(jnp.int32, (rows, WINDOW), 1) % 2 == 1
    gather_rows(piece, scratch, 0, (1, 2), segs)
    gather_rows(piece, scratch, rows, (3, 0), segs)
    re, im = transform(scratch, table_high, table_low)
    y_out[slot, :, :WINDOW] = re[:rows]
    y_out[slot, :, WINDOW:] = im[:rows]
    x_out[slot, :, :WINDOW] = re[:rows] + jnp.where(odd, -re[rows:], re[rows:])
    x_out[slot, :, WINDOW:] = im[:rows] + jnp.where(odd, -im[rows:], im[rows:])


def own_kernel(segs, *refs):
    pieces, (table_high, table_low, x_out, y_out, scratch) = refs[:-5], refs[-5:]
    for slot, piece in enumerate(pieces):
        own_transform(piece, slot, table_high, table_low, x_out, y_out, scratch, segs)


def far_transform(piece, table_high, table_low, y_out, scratch, segs):
    gather_rows(piece, scratch, 0, (1, 2), segs)
    y_re, y_im = transform(scratch, table_high, table_low)
    y_out[0, :, :WINDOW] = y_re
    y_out[0, :, WINDOW:] = y_im


def far_kernel(segs, piece, table_high, table_low, y_out, scratch):
    far_transform(piece, table_high, table_low, y_out, scratch, segs)


def level_kernel(segs, place, piece, table_high, table_low, x_in, y_in, *refs):
    del x_in, y_in
    ready, (x_out, y_out, spectrum, scratch) = refs[:-4], refs[-4:]
    me = place[0]
    own_transform(piece, OFFS - 1, table_high, table_low, x_out, y_out, scratch, segs)
    near_pairs(segs, me, x_out, y_out, spectrum)
    for slot, y_ref in enumerate(ready):
        for x_slot in range(OFFS):
            q = me ^ x_slot
            far_pair(segs, q, me ^ slot, x_out, x_slot, y_ref, spectrum, q * (OFFS * segs))


def ahead_kernel(
    segs, slot, place, piece, table_high, table_low, x_ref, _, spectrum, y_scratch, scratch
):
    far_transform(piece, table_high, table_low, y_scratch, scratch, segs)
    me = place[0]
    for x_slot in range(OFFS):
        q = me ^ x_slot
        far_pair(segs, q, me ^ slot, x_ref, x_slot, y_scratch, spectrum, q * (OFFS * segs))


def finish(segs, parts, dy, place, x_ref, y_ref, sums, t_high, t_low, outs, spectrum, held):
    me, my_part = place[0], place[1]
    tile = 2 * segs
    lag_dev = LAGS // parts
    count = OFFS * segs
    slots = (2 * dy, 2 * dy + 1)
    for index, x_slot in enumerate(slots):
        q = me ^ x_slot
        spectrum[pl.ds(index * count, count), :] = sums[
            pl.ds(pl.multiple_of(q * count, count), count), :
        ]
        far_pair(segs, q, me ^ (OFFS - 1), x_ref, x_slot, y_ref, spectrum, index * count)
    s_re, s_im = spectrum[:, :WINDOW], spectrum[:, WINDOW:]
    left = jnp.concatenate(
        [jnp.concatenate([s_re, -s_im], axis=1), jnp.concatenate([s_im, s_re], axis=1)], axis=0
    )
    corr = product(left, t_high[...], t_low[...])
    wide_half = lax.broadcasted_iota(jnp.int32, (tile, LAGS), 0) < segs
    for index in range(len(slots)):
        for o in range(0, OFFS, 2):
            row = (index * OFFS + o) * segs
            re = corr[row : row + tile]
            im = corr[len(slots) * count + row : len(slots) * count + row + tile]
            first = jnp.where(wide_half, re, swap_halves(im))
            second = jnp.where(wide_half, swap_halves(re), im)
            for t in range(parts):
                lanes = slice(t * lag_dev, (t + 1) * lag_dev)
                held[index * parts + t, pl.ds(o * tile, tile), :] = first[:, lanes]
                held[index * parts + t, pl.ds((o + 1) * tile, tile), :] = second[:, lanes]
    send, keeps = outs[0], outs[1:]
    for dt, keep in enumerate(keeps):
        there = lax.rem(my_part + dt, parts)
        keep[...] = held[there]
        send[dt] = held[parts + there]


def first_kernel(segs, parts, place, piece, table_high, table_low, x_ref, sums, t_high, t_low, *refs):
    (y_out, *outs), (scratch, spectrum, held) = refs[:-3], refs[-3:]
    far_transform(piece, table_high, table_low, y_out, scratch, segs)
    finish(segs, parts, 1, place, x_ref, y_out, sums, t_high, t_low, outs, spectrum, held)


def second_kernel(segs, parts, place, y_ref, x_ref, sums, t_high, t_low, *refs):
    outs, (spectrum, held) = refs[:-2], refs[-2:]
    finish(segs, parts, 0, place, x_ref, y_ref, sums, t_high, t_low, outs, spectrum, held)


def doppler_kernel(segs, keep_ref, recv_ref, *refs):
    others, (table_high, table_low, out_ref, scratch, sems) = refs[:-5], refs[-5:]
    tile = 2 * segs
    lag_dev = keep_ref.shape[1]
    stride = scratch.shape[0] // lag_dev
    per = DOPK // HALF
    table = jnp.concatenate([table_high[...], table_high[...], table_low[...]], axis=0)
    outs = []
    for o in range(OFFS):
        rows = pl.ds(o * tile, tile)
        tiles = [keep_ref[rows, :], recv_ref[0, rows, :]]
        for other in others:
            tiles += [other[0, rows, :], other[1, rows, :]]
        high, low = split(jnp.concatenate(tiles, axis=0))
        left = jnp.concatenate([high, low, high], axis=0)
        outs.append(
            lax.dot_general(
                left, table, (((0,), (0,)), ((), ())), preferred_element_type=jnp.float32
            )
        )
    lags = lag_dev // STORES
    copies = []
    for store in range(STORES):
        base = store * lags
        for o in range(OFFS):
            for c in range(2):
                for f in range(per):
                    where = base * stride + (c * OFFS + o) * per + f
                    first = c * DOPK + f * HALF
                    scratch[pl.ds(where, lags, stride=stride), :] = outs[o][
                        base : base + lags, first : first + HALF
                    ]
        span = pl.ds(base * stride, lags * stride)
        copies.append(pltpu.make_async_copy(scratch.at[span], out_ref.at[span], sems.at[store]))
        copies[-1].start()
    for copy in copies:
        copy.wait()


def doppler_table(sources, seg_dev, segs, scale):
    segment = jnp.concatenate(
        [part * seg_dev + slot * segs + jnp.arange(segs, dtype=jnp.int32) for slot, part in sources]
    )
    frequency = jnp.arange(DOPK, dtype=jnp.int32) - DOPK // 2
    angle = (
        2.0 * math.pi / DOPLEN
        * (segment[:, None] * frequency[None, :] % DOPLEN).astype(jnp.float32)
    )
    cos, sin = (jnp.cos(angle) * scale, jnp.sin(angle) * scale)
    cos = cos.reshape(len(sources), 1, segs, DOPK)
    sin = sin.reshape(len(sources), 1, segs, DOPK)
    table = jnp.concatenate(
        [jnp.concatenate([cos, -sin], axis=3), jnp.concatenate([sin, cos], axis=3)], axis=1
    ).reshape(2 * len(sources) * segs, 2 * DOPK)
    return split_table(table)


def per_device(count, parts, signals):
    rec_dev, length = signals.shape[1], signals.shape[2]
    seg_dev = length // SEG_LEN
    segs = seg_dev // OFFS
    assert rec_dev == 1 and count % OFFS == 0 and seg_dev % OFFS == 0
    me = lax.axis_index("rx") % OFFS
    my_part = lax.axis_index("tm")
    place = jnp.stack([me, my_part]).astype(jnp.int32)

    def move(value, flip, ahead=0, later=0):
        pairs = []
        for r in range(count):
            for t in range(parts):
                to = ((r ^ flip) + ahead) % count
                pairs.append((r * parts + t, to * parts + (t + later) % parts))
        return lax.ppermute(value, ("rx", "tm"), pairs)

    raw = signals.reshape(2, seg_dev * ROWS, HALF)

    cuts = [
        lax.dynamic_slice_in_dim(raw, (me ^ slot) * (segs * ROWS), segs * ROWS, axis=1)
        for slot in range(OFFS)
    ]
    own = [cuts[0]]
    own += [move(cuts[slot], slot) for slot in range(1, OFFS)]
    far = [
        move(own[slot], 0, ahead=OFFS)
        if slot in RELAYED
        else move(cuts[slot], slot, ahead=OFFS)
        for slot in range(OFFS)
    ]

    frequency = np.arange(WINDOW)
    high, low = halves(trig(np.arange(BLOCK), frequency))
    t_high, t_low = halves(trig(frequency, np.arange(LAGS) - HALF) / WINDOW)

    rows = BLOCKS * segs
    last = OFFS - 1
    spectra = jax.ShapeDtypeStruct((OFFS, rows, 2 * WINDOW), jnp.float32)
    spectrum = jax.ShapeDtypeStruct((1, rows, 2 * WINDOW), jnp.float32)
    sums = jax.ShapeDtypeStruct((OFFS * OFFS * segs, 2 * WINDOW), jnp.float32)
    own_rows = pltpu.VMEM((2 * rows, 2 * BLOCK), jnp.float32)
    far_rows = pltpu.VMEM((rows, 2 * BLOCK), jnp.float32)
    x_own, y_own = pl.pallas_call(
        functools.partial(own_kernel, segs),
        out_shape=(spectra, spectra),
        in_specs=[VMEM] * (last + 2),
        out_specs=(VMEM, VMEM),
        scratch_shapes=[own_rows],
        compiler_params=limit(6),
        name="own",
    )(*own[:last], high, low)
    ready = [
        pl.pallas_call(
            functools.partial(far_kernel, segs),
            out_shape=spectrum,
            in_specs=[VMEM] * 3,
            out_specs=VMEM,
            scratch_shapes=[far_rows],
            compiler_params=limit(4),
            name="far",
        )(piece, high, low)
        for piece in far[: last - 1]
    ]
    x_own, _, total = pl.pallas_call(
        functools.partial(level_kernel, segs),
        out_shape=(spectra, spectra, sums),
        in_specs=[SMEM] + [VMEM] * (5 + len(ready)),
        out_specs=(VMEM, VMEM, VMEM),
        scratch_shapes=[own_rows],
        input_output_aliases={4: 0, 5: 1},
        compiler_params=limit(6),
        name="level",
    )(place, own[last], high, low, x_own, y_own, *ready)
    total = pl.pallas_call(
        functools.partial(ahead_kernel, segs, last - 1),
        out_shape=sums,
        in_specs=[SMEM] + [VMEM] * 5,
        out_specs=VMEM,
        scratch_shapes=[pltpu.VMEM(spectrum.shape, jnp.float32), far_rows],
        input_output_aliases={5: 0},
        compiler_params=limit(4),
        name="ahead",
    )(place, far[last - 1], high, low, x_own, total)

    lag_dev = LAGS // parts
    piece_rows = OFFS * 2 * segs
    sources = []
    for dy in range(2):
        for dt in range(parts):
            slot, part = me ^ (2 * dy), (my_part - dt) % parts
            sources += [(slot, part), (slot ^ 1, part)]
    scale = 1.0 / math.sqrt(2.0 * SEG_LEN * seg_dev * parts)
    d_high, d_low, total = lax.optimization_barrier(
        (*doppler_table(sources, seg_dev, segs, scale), total)
    )
    keep = jax.ShapeDtypeStruct((piece_rows, lag_dev), jnp.float32)
    leaving = (jax.ShapeDtypeStruct((parts, piece_rows, lag_dev), jnp.float32),) + (keep,) * parts
    working = [
        pltpu.VMEM((2 * OFFS * segs, 2 * WINDOW), jnp.float32),
        pltpu.VMEM((2 * parts, piece_rows, lag_dev), jnp.float32),
    ]
    y_last, *crossing = pl.pallas_call(
        functools.partial(first_kernel, segs, parts),
        out_shape=(spectrum, *leaving),
        in_specs=[SMEM] + [VMEM] * 7,
        out_specs=(VMEM,) * (2 + parts),
        scratch_shapes=[far_rows] + working,
        compiler_params=limit(6),
        name="first",
    )(place, far[last], high, low, x_own, total, t_high, t_low)
    staying = pl.pallas_call(
        functools.partial(second_kernel, segs, parts),
        out_shape=leaving,
        in_specs=[SMEM] + [VMEM] * 5,
        out_specs=(VMEM,) * (1 + parts),
        scratch_shapes=working,
        compiler_params=limit(6),
        name="second",
    )(place, y_last, x_own, total, t_high, t_low)
    got = {1: move(crossing[0], 1), 0: move(staying[0], 1)}
    kept = {1: crossing[1:], 0: staying[1:]}
    keep, recv = kept[0][0], got[0]
    others = [
        move(jnp.stack([kept[dy][dt], got[dy][dt]]), 2 * dy, later=dt)
        for dy in range(2)
        for dt in range(parts)
        if dy or dt
    ]
    out_rows = lag_dev * 2 * OFFS * DOPK // HALF
    out = pl.pallas_call(
        functools.partial(doppler_kernel, segs),
        out_shape=jax.ShapeDtypeStruct((out_rows, HALF), jnp.float32),
        in_specs=[VMEM] * (len(others) + 4),
        out_specs=ANY,
        scratch_shapes=[
            pltpu.VMEM((out_rows, HALF), jnp.float32),
            pltpu.SemaphoreType.DMA((STORES,)),
        ],
        compiler_params=limit(6),
        name="doppler",
    )(keep, recv, *others, d_high, d_low)
    return out.reshape(lag_dev, 2, 1, OFFS, 1, DOPK)


def solution(mesh):
    count, parts = mesh.shape["rx"], mesh.shape["tm"]

    def body(signals):
        return per_device(count, parts, signals)

    return jax.shard_map(
        body,
        mesh=mesh,
        in_specs=(P(None, "rx", "tm"),),
        out_specs=P("tm", None, "rx", None, None, None),
        check_vma=False,
    )
```

```python
import functools
import math

import jax
import jax.numpy as jnp
import numpy as np
from jax import lax
from jax.experimental import pallas as pl
from jax.experimental.pallas import tpu as pltpu
from jax.sharding import PartitionSpec as P


SEG_LEN = 4096
LAGS = 256
DOPLEN = 512
DOPK = 256
OFFS = 4

HALF = LAGS // 2
BLOCK = LAGS
WINDOW = 2 * LAGS
BLOCKS = SEG_LEN // BLOCK
ROWS = SEG_LEN // HALF
CLASSES = 4
WIDE = WINDOW // CLASSES * 2
STORES = 4

VMEM = pl.BlockSpec(memory_space=pltpu.VMEM)
ANY = pl.BlockSpec(memory_space=pl.ANY)


def limit(mib):
    return pltpu.CompilerParams(vmem_limit_bytes=mib << 20)


RELAYED = (0, 2, 3)


def halves(table):
    high = table.astype(jnp.bfloat16)
    return jnp.asarray(high), jnp.asarray((table - high.astype(np.float64)).astype(jnp.bfloat16))


def forward_table():
    blocks = []
    for first in range(CLASSES):
        turns = np.outer(np.arange(HALF), np.arange(first, WINDOW, CLASSES)) % WINDOW
        cos, sin = np.cos(2.0 * math.pi / WINDOW * turns), np.sin(2.0 * math.pi / WINDOW * turns)
        blocks.append(np.block([[cos, -sin], [sin, cos]]))
    return np.concatenate(blocks, axis=0)


def inverse_table():
    blocks = []
    for first in range(CLASSES):
        turns = np.outer(np.arange(first, WINDOW, CLASSES), np.arange(HALF)) % WINDOW
        cos, sin = np.cos(2.0 * math.pi / WINDOW * turns), np.sin(2.0 * math.pi / WINDOW * turns)
        blocks.append(np.block([[cos, sin], [-sin, cos]]) / WINDOW)
    return np.concatenate(blocks, axis=0)


def split(value):
    high = value.astype(jnp.bfloat16)
    low = (value - high.astype(jnp.float32)).astype(jnp.bfloat16)
    return high, low


def split_table(value):
    high = lax.reduce_precision(value, exponent_bits=8, mantissa_bits=7)
    return high.astype(jnp.bfloat16), (value - high).astype(jnp.bfloat16)


def product(left, table_high, table_low):
    high, low = split(left)
    count = left.shape[0]
    both = jnp.dot(
        jnp.concatenate([high, low], axis=0), table_high, preferred_element_type=jnp.float32
    )
    rest = jnp.dot(high, table_low, preferred_element_type=jnp.float32)
    return both[:count] + both[count:] + rest


def gather_rows(piece_ref, scratch, row, firsts, segs):
    for plane in range(2):
        for position, first in enumerate(firsts):
            column = pl.ds(plane * BLOCK + position * HALF, HALF)
            for block in range(BLOCKS):
                half = (2 * block + first) % ROWS
                scratch[pl.ds(row + block * segs, segs), column] = piece_ref[
                    plane, pl.ds(half, segs, stride=ROWS), :
                ]


def add_turned(total, value, power):
    (a, b), (c, d) = total, value
    return ((a + c, b + d), (a + d, b - c), (a - c, b - d), (a - d, b + c))[power % 4]


def table_block(table_ref, kind):
    return table_ref[kind * WIDE : (kind + 1) * WIDE, :]


def transform(scratch, table_high, table_low, store, count, whole):
    def part(first, place):
        rows = slice(first, first + count)
        real, imag = place * HALF, BLOCK + place * HALF
        return scratch[rows, real : real + HALF], scratch[rows, imag : imag + HALF]

    odd, even = part(0, 0), part(0, 1)
    for kind in range(CLASSES):
        value = add_turned(odd, even, kind)
        left = jnp.concatenate(value, axis=1)
        if whole:
            value = add_turned(value, part(count, 1), -kind)
            value = add_turned(value, part(count, 0), 2 * kind)
            left = jnp.concatenate([left, jnp.concatenate(value, axis=1)], axis=0)
        out = product(left, table_block(table_high, kind), table_block(table_low, kind))
        store(pl.ds(kind * WIDE, WIDE), out)


def position(parts):
    return lax.rem(lax.axis_index("rx"), OFFS), lax.axis_index("tm") if parts > 1 else 0


def swap_halves(value):
    return pltpu.roll(value, value.shape[0] // 2, axis=0)


def pair_sum(x_ref, x_slot, y_ref, y_slot, column, tile):
    re, im = None, None
    for row in range(0, x_ref.shape[1], tile):
        rows = pl.ds(row, tile)
        x_re = x_ref[x_slot, rows, pl.ds(column, HALF)]
        x_im = x_ref[x_slot, rows, pl.ds(column + HALF, HALF)]
        y_re = y_ref[y_slot, rows, pl.ds(column, HALF)]
        y_im = y_ref[y_slot, rows, pl.ds(column + HALF, HALF)]
        more_re = x_re * y_re + x_im * y_im
        more_im = x_im * y_re - x_re * y_im
        re, im = (more_re, more_im) if re is None else (re + more_re, im + more_im)
    return re, im


def near_pairs(segs, me, x_ref, y_ref, spectrum):
    tile = 2 * segs
    first_half = lax.broadcasted_iota(jnp.int32, (tile, HALF), 0) < segs
    zero = jnp.zeros((tile, HALF), jnp.float32)
    for q in range(OFFS):
        for column in range(0, 2 * WINDOW, WIDE):
            sums = [
                pair_sum(x_ref, q ^ me, y_ref, (q - 1 - o) ^ me, column, tile)
                if o < q
                else (zero, zero)
                for o in range(OFFS)
            ]
            for o in range(0, OFFS, 2):
                rows = pl.ds((q * OFFS + o) * segs, tile)
                for part, base in ((0, 0), (1, HALF)):
                    a, b = sums[o][part], sums[o + 1][part]
                    spectrum[rows, pl.ds(base + column, HALF)] = jnp.where(
                        first_half, a, b
                    ) + swap_halves(jnp.where(first_half, b, a))


def far_pair(segs, q, r, x_ref, x_slot, y_ref, spectrum, first_row):
    tile = 2 * segs
    o = q + (OFFS - 1) - r

    @pl.when(q <= r)
    def _():
        second = lax.broadcasted_iota(jnp.int32, (tile, HALF), 0) >= segs
        mine = second == (lax.rem(o, 2) == 1)
        rows = pl.ds(pl.multiple_of(first_row + (o - lax.rem(o, 2)) * segs, tile), tile)
        for column in range(0, 2 * WINDOW, WIDE):
            sums = pair_sum(x_ref, x_slot, y_ref, 0, column, tile)
            for value, base in zip(sums, (0, HALF)):
                columns = pl.ds(base + column, HALF)
                total = value + swap_halves(value)
                spectrum[rows, columns] = spectrum[rows, columns] + jnp.where(mine, total, 0.0)


def own_transform(piece, slot, table_high, table_low, x_out, y_out, scratch, segs):
    rows = BLOCKS * segs
    gather_rows(piece, scratch, 0, (1, 2), segs)
    gather_rows(piece, scratch, rows, (3, 0), segs)

    def store(columns, value):
        y_out[slot, :, columns] = value[:rows]
        x_out[slot, :, columns] = value[rows:]

    transform(scratch, table_high, table_low, store, rows, True)


def own_kernel(segs, *refs):
    pieces, (table_high, table_low, x_out, y_out, scratch) = refs[:-5], refs[-5:]
    for slot, piece in enumerate(pieces):
        own_transform(piece, slot, table_high, table_low, x_out, y_out, scratch, segs)


def far_transform(piece, table_high, table_low, y_out, scratch, segs):
    gather_rows(piece, scratch, 0, (1, 2), segs)

    def store(columns, value):
        y_out[0, :, columns] = value

    transform(scratch, table_high, table_low, store, BLOCKS * segs, False)


def far_kernel(segs, piece, table_high, table_low, y_out, scratch):
    far_transform(piece, table_high, table_low, y_out, scratch, segs)


def level_kernel(segs, piece, table_high, table_low, x_in, y_in, *refs):
    del x_in, y_in
    ready, (x_out, y_out, spectrum, scratch) = refs[:-4], refs[-4:]
    me, _ = position(1)
    own_transform(piece, OFFS - 1, table_high, table_low, x_out, y_out, scratch, segs)
    near_pairs(segs, me, x_out, y_out, spectrum)
    for slot, y_ref in enumerate(ready):
        for x_slot in range(OFFS):
            q = me ^ x_slot
            far_pair(segs, q, me ^ slot, x_out, x_slot, y_ref, spectrum, q * (OFFS * segs))


def ahead_kernel(
    segs, slot, piece, table_high, table_low, x_ref, _, spectrum, y_scratch, scratch
):
    far_transform(piece, table_high, table_low, y_scratch, scratch, segs)
    me, _ = position(1)
    for x_slot in range(OFFS):
        q = me ^ x_slot
        far_pair(segs, q, me ^ slot, x_ref, x_slot, y_scratch, spectrum, q * (OFFS * segs))


def finish(segs, parts, dy, x_ref, y_ref, sums, t_high, t_low, outs, spectrum, held):
    me, my_part = position(parts)
    tile = 2 * segs
    lag_dev = LAGS // parts
    count = OFFS * segs
    slots = (2 * dy, 2 * dy + 1)
    for index, x_slot in enumerate(slots):
        q = me ^ x_slot
        spectrum[pl.ds(index * count, count), :] = sums[
            pl.ds(pl.multiple_of(q * count, count), count), :
        ]
        far_pair(segs, q, me ^ (OFFS - 1), x_ref, x_slot, y_ref, spectrum, index * count)
    early, late = None, None
    for kind in range(CLASSES):
        out = product(
            spectrum[:, kind * WIDE : (kind + 1) * WIDE],
            table_block(t_high, kind),
            table_block(t_low, kind),
        )
        value = (out[:, :HALF], out[:, HALF:])
        early = add_turned(early, value, kind) if early else value
        late = add_turned(late, value, 0) if late else value
    corr_re = jnp.concatenate([early[0], late[0]], axis=1)
    corr_im = jnp.concatenate([early[1], late[1]], axis=1)
    wide_half = lax.broadcasted_iota(jnp.int32, (tile, LAGS), 0) < segs
    for index in range(len(slots)):
        for o in range(0, OFFS, 2):
            row = (index * OFFS + o) * segs
            re, im = corr_re[row : row + tile], corr_im[row : row + tile]
            first = jnp.where(wide_half, re, swap_halves(im))
            second = jnp.where(wide_half, swap_halves(re), im)
            for t in range(parts):
                lanes = slice(t * lag_dev, (t + 1) * lag_dev)
                held[index * parts + t, pl.ds(o * tile, tile), :] = first[:, lanes]
                held[index * parts + t, pl.ds((o + 1) * tile, tile), :] = second[:, lanes]
    send, keeps = outs[0], outs[1:]
    for dt, keep in enumerate(keeps):
        there = lax.rem(my_part + dt, parts)
        keep[...] = held[there]
        send[dt] = held[parts + there]


def first_kernel(segs, parts, piece, table_high, table_low, x_ref, sums, t_high, t_low, *refs):
    (y_out, *outs), (scratch, spectrum, held) = refs[:-3], refs[-3:]
    far_transform(piece, table_high, table_low, y_out, scratch, segs)
    finish(segs, parts, 1, x_ref, y_out, sums, t_high, t_low, outs, spectrum, held)


def second_kernel(segs, parts, y_ref, x_ref, sums, t_high, t_low, *refs):
    outs, (spectrum, held) = refs[:-2], refs[-2:]
    finish(segs, parts, 0, x_ref, y_ref, sums, t_high, t_low, outs, spectrum, held)


def doppler_kernel(segs, keep_ref, recv_ref, *refs):
    others, (table_high, table_low, out_ref, scratch, sems) = refs[:-5], refs[-5:]
    tile = 2 * segs
    lag_dev = keep_ref.shape[1]
    stride = scratch.shape[0] // lag_dev
    per = DOPK // HALF
    table = jnp.concatenate([table_high[...], table_high[...], table_low[...]], axis=0)
    outs = []
    for o in range(OFFS):
        rows = pl.ds(o * tile, tile)
        tiles = [keep_ref[rows, :], recv_ref[0, rows, :]]
        for other in others:
            tiles += [other[0, rows, :], other[1, rows, :]]
        high, low = split(jnp.concatenate(tiles, axis=0))
        left = jnp.concatenate([high, low, high], axis=0)
        outs.append(
            lax.dot_general(
                left, table, (((0,), (0,)), ((), ())), preferred_element_type=jnp.float32
            )
        )
    lags = lag_dev // STORES
    copies = []
    for store in range(STORES):
        base = store * lags
        for o in range(OFFS):
            for c in range(2):
                for f in range(per):
                    where = base * stride + (c * OFFS + o) * per + f
                    first = c * DOPK + f * HALF
                    scratch[pl.ds(where, lags, stride=stride), :] = outs[o][
                        base : base + lags, first : first + HALF
                    ]
        span = pl.ds(base * stride, lags * stride)
        copies.append(pltpu.make_async_copy(scratch.at[span], out_ref.at[span], sems.at[store]))
        copies[-1].start()
    for copy in copies:
        copy.wait()


def doppler_table(sources, seg_dev, segs, scale):
    segment = jnp.concatenate(
        [part * seg_dev + slot * segs + jnp.arange(segs, dtype=jnp.int32) for slot, part in sources]
    )
    frequency = jnp.arange(DOPK, dtype=jnp.int32) - DOPK // 2
    angle = (
        2.0 * math.pi / DOPLEN
        * (segment[:, None] * frequency[None, :] % DOPLEN).astype(jnp.float32)
    )
    cos, sin = (jnp.cos(angle) * scale, jnp.sin(angle) * scale)
    cos = cos.reshape(len(sources), 1, segs, DOPK)
    sin = sin.reshape(len(sources), 1, segs, DOPK)
    table = jnp.concatenate(
        [jnp.concatenate([cos, -sin], axis=3), jnp.concatenate([sin, cos], axis=3)], axis=1
    ).reshape(2 * len(sources) * segs, 2 * DOPK)
    return split_table(table)


def per_device(count, parts, signals):
    rec_dev, length = signals.shape[1], signals.shape[2]
    seg_dev = length // SEG_LEN
    segs = seg_dev // OFFS
    assert rec_dev == 1 and count % OFFS == 0 and seg_dev % OFFS == 0
    me = lax.axis_index("rx") % OFFS
    my_part = lax.axis_index("tm")

    def move(value, flip, ahead=0, later=0):
        pairs = []
        for r in range(count):
            for t in range(parts):
                to = ((r ^ flip) + ahead) % count
                pairs.append((r * parts + t, to * parts + (t + later) % parts))
        return lax.ppermute(value, ("rx", "tm"), pairs)

    raw = signals.reshape(2, seg_dev * ROWS, HALF)

    cuts = [
        lax.dynamic_slice_in_dim(raw, (me ^ slot) * (segs * ROWS), segs * ROWS, axis=1)
        for slot in range(OFFS)
    ]
    own = [cuts[0]]
    own += [move(cuts[slot], slot) for slot in range(1, OFFS)]
    far = [
        move(own[slot], 0, ahead=OFFS)
        if slot in RELAYED
        else move(cuts[slot], slot, ahead=OFFS)
        for slot in range(OFFS)
    ]

    high, low = halves(forward_table())
    t_high, t_low = halves(inverse_table())

    rows = BLOCKS * segs
    last = OFFS - 1
    spectra = jax.ShapeDtypeStruct((OFFS, rows, 2 * WINDOW), jnp.float32)
    spectrum = jax.ShapeDtypeStruct((1, rows, 2 * WINDOW), jnp.float32)
    sums = jax.ShapeDtypeStruct((OFFS * OFFS * segs, 2 * WINDOW), jnp.float32)
    own_rows = pltpu.VMEM((2 * rows, 2 * BLOCK), jnp.float32)
    far_rows = pltpu.VMEM((rows, 2 * BLOCK), jnp.float32)
    x_own, y_own = pl.pallas_call(
        functools.partial(own_kernel, segs),
        out_shape=(spectra, spectra),
        in_specs=[VMEM] * (last + 2),
        out_specs=(VMEM, VMEM),
        scratch_shapes=[own_rows],
        compiler_params=limit(6),
        name="own",
    )(*own[:last], high, low)
    ready = [
        pl.pallas_call(
            functools.partial(far_kernel, segs),
            out_shape=spectrum,
            in_specs=[VMEM] * 3,
            out_specs=VMEM,
            scratch_shapes=[far_rows],
            compiler_params=limit(4),
            name="far",
        )(piece, high, low)
        for piece in far[: last - 1]
    ]
    x_own, _, total = pl.pallas_call(
        functools.partial(level_kernel, segs),
        out_shape=(spectra, spectra, sums),
        in_specs=[VMEM] * (5 + len(ready)),
        out_specs=(VMEM, VMEM, VMEM),
        scratch_shapes=[own_rows],
        input_output_aliases={3: 0, 4: 1},
        compiler_params=limit(6),
        name="level",
    )(own[last], high, low, x_own, y_own, *ready)
    total = pl.pallas_call(
        functools.partial(ahead_kernel, segs, last - 1),
        out_shape=sums,
        in_specs=[VMEM] * 5,
        out_specs=VMEM,
        scratch_shapes=[pltpu.VMEM(spectrum.shape, jnp.float32), far_rows],
        input_output_aliases={4: 0},
        compiler_params=limit(4),
        name="ahead",
    )(far[last - 1], high, low, x_own, total)

    lag_dev = LAGS // parts
    piece_rows = OFFS * 2 * segs
    sources = []
    for dy in range(2):
        for dt in range(parts):
            slot, part = me ^ (2 * dy), (my_part - dt) % parts
            sources += [(slot, part), (slot ^ 1, part)]
    scale = 1.0 / math.sqrt(2.0 * SEG_LEN * seg_dev * parts)
    d_high, d_low, total = lax.optimization_barrier(
        (*doppler_table(sources, seg_dev, segs, scale), total)
    )
    keep = jax.ShapeDtypeStruct((piece_rows, lag_dev), jnp.float32)
    leaving = (jax.ShapeDtypeStruct((parts, piece_rows, lag_dev), jnp.float32),) + (keep,) * parts
    working = [
        pltpu.VMEM((2 * OFFS * segs, 2 * WINDOW), jnp.float32),
        pltpu.VMEM((2 * parts, piece_rows, lag_dev), jnp.float32),
    ]
    y_last, *crossing = pl.pallas_call(
        functools.partial(first_kernel, segs, parts),
        out_shape=(spectrum, *leaving),
        in_specs=[VMEM] * 7,
        out_specs=(VMEM,) * (2 + parts),
        scratch_shapes=[far_rows] + working,
        compiler_params=limit(6),
        name="first",
    )(far[last], high, low, x_own, total, t_high, t_low)
    staying = pl.pallas_call(
        functools.partial(second_kernel, segs, parts),
        out_shape=leaving,
        in_specs=[VMEM] * 5,
        out_specs=(VMEM,) * (1 + parts),
        scratch_shapes=working,
        compiler_params=limit(6),
        name="second",
    )(y_last, x_own, total, t_high, t_low)
    got = {1: move(crossing[0], 1), 0: move(staying[0], 1)}
    kept = {1: crossing[1:], 0: staying[1:]}
    keep, recv = kept[0][0], got[0]
    others = [
        move(jnp.stack([kept[dy][dt], got[dy][dt]]), 2 * dy, later=dt)
        for dy in range(2)
        for dt in range(parts)
        if dy or dt
    ]
    out_rows = lag_dev * 2 * OFFS * DOPK // HALF
    out = pl.pallas_call(
        functools.partial(doppler_kernel, segs),
        out_shape=jax.ShapeDtypeStruct((out_rows, HALF), jnp.float32),
        in_specs=[VMEM] * (len(others) + 4),
        out_specs=ANY,
        scratch_shapes=[
            pltpu.VMEM((out_rows, HALF), jnp.float32),
            pltpu.SemaphoreType.DMA((STORES,)),
        ],
        compiler_params=limit(6),
        name="doppler",
    )(keep, recv, *others, d_high, d_low)
    return out.reshape(lag_dev, 2, 1, OFFS, 1, DOPK)


def solution(mesh):
    count, parts = mesh.shape["rx"], mesh.shape["tm"]

    def body(signals):
        return per_device(count, parts, signals)

    return jax.shard_map(
        body,
        mesh=mesh,
        in_specs=(P(None, "rx", "tm"),),
        out_specs=P("tm", None, "rx", None, None, None),
        check_vma=False,
    )
```

```python
import functools
import math

import jax
import jax.numpy as jnp
import numpy as np
from jax import lax
from jax.experimental import pallas as pl
from jax.experimental.pallas import tpu as pltpu
from jax.sharding import PartitionSpec as P


SEG_LEN = 4096
LAGS = 256
DOPLEN = 512
DOPK = 256
OFFS = 4

HALF = LAGS // 2
BLOCK = LAGS
WINDOW = 2 * LAGS
BLOCKS = SEG_LEN // BLOCK
ROWS = SEG_LEN // HALF
CLASSES = 4
WIDE = WINDOW // CLASSES * 2
STORES = 4

VMEM = pl.BlockSpec(memory_space=pltpu.VMEM)
ANY = pl.BlockSpec(memory_space=pl.ANY)


def limit(mib):
    return pltpu.CompilerParams(vmem_limit_bytes=mib << 20)


RELAYED = (0, 2, 3)


def halves(table):
    high = table.astype(jnp.bfloat16)
    return jnp.asarray(high), jnp.asarray((table - high.astype(np.float64)).astype(jnp.bfloat16))


def forward_table():
    blocks = []
    for first in range(CLASSES):
        turns = np.outer(np.arange(HALF), np.arange(first, WINDOW, CLASSES)) % WINDOW
        cos, sin = np.cos(2.0 * math.pi / WINDOW * turns), np.sin(2.0 * math.pi / WINDOW * turns)
        blocks.append(np.block([[cos, -sin], [sin, cos]]))
    return np.concatenate(blocks, axis=0)


def inverse_table():
    blocks = []
    for first in range(CLASSES):
        turns = np.outer(np.arange(first, WINDOW, CLASSES), np.arange(HALF)) % WINDOW
        cos, sin = np.cos(2.0 * math.pi / WINDOW * turns), np.sin(2.0 * math.pi / WINDOW * turns)
        blocks.append(np.block([[cos, sin], [-sin, cos]]) / WINDOW)
    return np.concatenate(blocks, axis=0)


def split(value):
    high = value.astype(jnp.bfloat16)
    low = (value - high.astype(jnp.float32)).astype(jnp.bfloat16)
    return high, low


def split_table(value):
    high = lax.reduce_precision(value, exponent_bits=8, mantissa_bits=7)
    return high.astype(jnp.bfloat16), (value - high).astype(jnp.bfloat16)


def product(left, table_high, table_low):
    high, low = split(left)
    count = left.shape[0]
    both = jnp.dot(
        jnp.concatenate([high, low], axis=0), table_high, preferred_element_type=jnp.float32
    )
    rest = jnp.dot(high, table_low, preferred_element_type=jnp.float32)
    return both[:count] + both[count:] + rest


def gather_rows(piece_ref, scratch, row, firsts, segs):
    for plane in range(2):
        for position, first in enumerate(firsts):
            column = pl.ds(plane * BLOCK + position * HALF, HALF)
            for block in range(BLOCKS):
                half = (2 * block + first) % ROWS
                scratch[pl.ds(row + block * segs, segs), column] = piece_ref[
                    plane, pl.ds(half, segs, stride=ROWS), :
                ]


def add_turned(total, value, power):
    (a, b), (c, d) = total, value
    return ((a + c, b + d), (a + d, b - c), (a - c, b - d), (a - d, b + c))[power % 4]


def table_block(table_ref, kind):
    return table_ref[kind * WIDE : (kind + 1) * WIDE, :]


def transform(scratch, table_high, table_low, store, count, whole):
    def part(first, place):
        rows = slice(first, first + count)
        real, imag = place * HALF, BLOCK + place * HALF
        return scratch[rows, real : real + HALF], scratch[rows, imag : imag + HALF]

    odd, even = part(0, 0), part(0, 1)
    for kind in range(CLASSES):
        value = add_turned(odd, even, kind)
        left = jnp.concatenate(value, axis=1)
        if whole:
            value = add_turned(value, part(count, 1), -kind)
            value = add_turned(value, part(count, 0), 2 * kind)
            left = jnp.concatenate([left, jnp.concatenate(value, axis=1)], axis=0)
        out = product(left, table_block(table_high, kind), table_block(table_low, kind))
        store(pl.ds(kind * WIDE, WIDE), out)


def position(parts):
    return lax.rem(lax.axis_index("rx"), OFFS), lax.axis_index("tm") if parts > 1 else 0


def swap_halves(value):
    return pltpu.roll(value, value.shape[0] // 2, axis=0)


def pair_sum(x_ref, x_slot, y_ref, y_slot, column, tile):
    re, im = None, None
    for row in range(0, x_ref.shape[1], tile):
        rows = pl.ds(row, tile)
        x_re = x_ref[x_slot, rows, pl.ds(column, HALF)]
        x_im = x_ref[x_slot, rows, pl.ds(column + HALF, HALF)]
        y_re = y_ref[y_slot, rows, pl.ds(column, HALF)]
        y_im = y_ref[y_slot, rows, pl.ds(column + HALF, HALF)]
        more_re = x_re * y_re + x_im * y_im
        more_im = x_im * y_re - x_re * y_im
        re, im = (more_re, more_im) if re is None else (re + more_re, im + more_im)
    return re, im


def near_pairs(segs, me, x_ref, y_ref, spectrum):
    tile = 2 * segs
    first_half = lax.broadcasted_iota(jnp.int32, (tile, HALF), 0) < segs
    zero = jnp.zeros((tile, HALF), jnp.float32)
    for q in range(OFFS):
        for column in range(0, 2 * WINDOW, WIDE):
            sums = [
                pair_sum(x_ref, q ^ me, y_ref, (q - 1 - o) ^ me, column, tile)
                if o < q
                else (zero, zero)
                for o in range(OFFS)
            ]
            for o in range(0, OFFS, 2):
                rows = pl.ds((q * OFFS + o) * segs, tile)
                for part, base in ((0, 0), (1, HALF)):
                    a, b = sums[o][part], sums[o + 1][part]
                    spectrum[rows, pl.ds(base + column, HALF)] = jnp.where(
                        first_half, a, b
                    ) + swap_halves(jnp.where(first_half, b, a))


def far_pair(segs, q, r, x_ref, x_slot, y_ref, spectrum, first_row):
    tile = 2 * segs
    o = q + (OFFS - 1) - r

    @pl.when(q <= r)
    def _():
        second = lax.broadcasted_iota(jnp.int32, (tile, HALF), 0) >= segs
        mine = second == (lax.rem(o, 2) == 1)
        rows = pl.ds(pl.multiple_of(first_row + (o - lax.rem(o, 2)) * segs, tile), tile)
        for column in range(0, 2 * WINDOW, WIDE):
            sums = pair_sum(x_ref, x_slot, y_ref, 0, column, tile)
            for value, base in zip(sums, (0, HALF)):
                columns = pl.ds(base + column, HALF)
                total = value + swap_halves(value)
                spectrum[rows, columns] = spectrum[rows, columns] + jnp.where(mine, total, 0.0)


def own_transform(piece, slot, table_high, table_low, x_out, y_out, scratch, segs):
    rows = BLOCKS * segs
    gather_rows(piece, scratch, 0, (1, 2), segs)
    gather_rows(piece, scratch, rows, (3, 0), segs)

    def store(columns, value):
        y_out[slot, :, columns] = value[:rows]
        x_out[slot, :, columns] = value[rows:]

    transform(scratch, table_high, table_low, store, rows, True)


def own_kernel(segs, *refs):
    pieces, (table_high, table_low, x_out, y_out, scratch) = refs[:-5], refs[-5:]
    for slot, piece in enumerate(pieces):
        own_transform(piece, slot, table_high, table_low, x_out, y_out, scratch, segs)


def far_transform(piece, table_high, table_low, y_out, scratch, segs):
    gather_rows(piece, scratch, 0, (1, 2), segs)

    def store(columns, value):
        y_out[0, :, columns] = value

    transform(scratch, table_high, table_low, store, BLOCKS * segs, False)


def far_kernel(segs, piece, table_high, table_low, y_out, scratch):
    far_transform(piece, table_high, table_low, y_out, scratch, segs)


def level_kernel(segs, piece, table_high, table_low, x_in, y_in, *refs):
    del x_in, y_in
    ready, (x_out, y_out, spectrum, scratch) = refs[:-4], refs[-4:]
    me, _ = position(1)
    own_transform(piece, OFFS - 1, table_high, table_low, x_out, y_out, scratch, segs)
    near_pairs(segs, me, x_out, y_out, spectrum)
    for slot, y_ref in enumerate(ready):
        for x_slot in range(OFFS):
            q = me ^ x_slot
            far_pair(segs, q, me ^ slot, x_out, x_slot, y_ref, spectrum, q * (OFFS * segs))


def ahead_kernel(
    segs, slot, piece, table_high, table_low, x_ref, _, spectrum, y_scratch, scratch
):
    far_transform(piece, table_high, table_low, y_scratch, scratch, segs)
    me, _ = position(1)
    for x_slot in range(OFFS):
        q = me ^ x_slot
        far_pair(segs, q, me ^ slot, x_ref, x_slot, y_scratch, spectrum, q * (OFFS * segs))


def last_kernel(segs, parts, piece, table_high, table_low, x_ref, sums, t_high, t_low, *refs):
    outs, (y_ref, scratch, spectrum, held) = refs[:-4], refs[-4:]
    far_transform(piece, table_high, table_low, y_ref, scratch, segs)
    me, my_part = position(parts)
    tile = 2 * segs
    lag_dev = LAGS // parts
    count = OFFS * segs
    for x_slot in range(OFFS):
        q = me ^ x_slot
        spectrum[pl.ds(x_slot * count, count), :] = sums[
            pl.ds(pl.multiple_of(q * count, count), count), :
        ]
        far_pair(segs, q, me ^ (OFFS - 1), x_ref, x_slot, y_ref, spectrum, x_slot * count)
    early, late = None, None
    for kind in range(CLASSES):
        out = product(
            spectrum[:, kind * WIDE : (kind + 1) * WIDE],
            table_block(t_high, kind),
            table_block(t_low, kind),
        )
        value = (out[:, :HALF], out[:, HALF:])
        early = add_turned(early, value, kind) if early else value
        late = add_turned(late, value, 0) if late else value
    corr_re = jnp.concatenate([early[0], late[0]], axis=1)
    corr_im = jnp.concatenate([early[1], late[1]], axis=1)
    wide_half = lax.broadcasted_iota(jnp.int32, (tile, LAGS), 0) < segs
    for index in range(OFFS):
        for o in range(0, OFFS, 2):
            row = (index * OFFS + o) * segs
            re, im = corr_re[row : row + tile], corr_im[row : row + tile]
            first = jnp.where(wide_half, re, swap_halves(im))
            second = jnp.where(wide_half, swap_halves(re), im)
            for t in range(parts):
                lanes = slice(t * lag_dev, (t + 1) * lag_dev)
                held[index * parts + t, pl.ds(o * tile, tile), :] = first[:, lanes]
                held[index * parts + t, pl.ds((o + 1) * tile, tile), :] = second[:, lanes]
    send, keeps, crossing = outs[0], outs[1 : 1 + parts], outs[1 + parts :]
    for dt in range(parts):
        there = lax.rem(my_part + dt, parts)
        keeps[dt][...] = held[there]
        send[dt] = held[parts + there]
        crossing[dt][0] = held[2 * parts + there]
        crossing[dt][1] = held[3 * parts + there]


def turn_kernel(*refs):
    for index, piece in enumerate(refs[:-1]):
        refs[-1][index] = piece[1]


def doppler_kernel(segs, parts, keep_ref, recv_ref, *refs):
    straight, crossing = refs[: parts - 1], refs[parts - 1 : 2 * parts - 1]
    cross_ref, table_high, table_low, out_ref, scratch, sems = refs[2 * parts - 1 :]
    tile = 2 * segs
    lag_dev = keep_ref.shape[1]
    stride = scratch.shape[0] // lag_dev
    per = DOPK // HALF
    table = jnp.concatenate([table_high[...], table_high[...], table_low[...]], axis=0)
    outs = []
    for o in range(OFFS):
        rows = pl.ds(o * tile, tile)
        tiles = [keep_ref[rows, :], recv_ref[0, rows, :]]
        for other in straight:
            tiles += [other[0, rows, :], other[1, rows, :]]
        for dt, other in enumerate(crossing):
            tiles += [other[0, rows, :], cross_ref[dt, rows, :]]
        high, low = split(jnp.concatenate(tiles, axis=0))
        left = jnp.concatenate([high, low, high], axis=0)
        outs.append(
            lax.dot_general(
                left, table, (((0,), (0,)), ((), ())), preferred_element_type=jnp.float32
            )
        )
    lags = lag_dev // STORES
    copies = []
    for store in range(STORES):
        base = store * lags
        for o in range(OFFS):
            for c in range(2):
                for f in range(per):
                    where = base * stride + (c * OFFS + o) * per + f
                    first = c * DOPK + f * HALF
                    scratch[pl.ds(where, lags, stride=stride), :] = outs[o][
                        base : base + lags, first : first + HALF
                    ]
        span = pl.ds(base * stride, lags * stride)
        copies.append(pltpu.make_async_copy(scratch.at[span], out_ref.at[span], sems.at[store]))
        copies[-1].start()
    for copy in copies:
        copy.wait()


def doppler_table(sources, seg_dev, segs, scale):
    segment = jnp.concatenate(
        [part * seg_dev + slot * segs + jnp.arange(segs, dtype=jnp.int32) for slot, part in sources]
    )
    frequency = jnp.arange(DOPK, dtype=jnp.int32) - DOPK // 2
    angle = (
        2.0 * math.pi / DOPLEN
        * (segment[:, None] * frequency[None, :] % DOPLEN).astype(jnp.float32)
    )
    cos, sin = (jnp.cos(angle) * scale, jnp.sin(angle) * scale)
    cos = cos.reshape(len(sources), 1, segs, DOPK)
    sin = sin.reshape(len(sources), 1, segs, DOPK)
    table = jnp.concatenate(
        [jnp.concatenate([cos, -sin], axis=3), jnp.concatenate([sin, cos], axis=3)], axis=1
    ).reshape(2 * len(sources) * segs, 2 * DOPK)
    return split_table(table)


def per_device(count, parts, signals):
    rec_dev, length = signals.shape[1], signals.shape[2]
    seg_dev = length // SEG_LEN
    segs = seg_dev // OFFS
    assert rec_dev == 1 and count % OFFS == 0 and seg_dev % OFFS == 0
    me = lax.axis_index("rx") % OFFS
    my_part = lax.axis_index("tm")

    def move(value, flip, ahead=0, later=0):
        pairs = []
        for r in range(count):
            for t in range(parts):
                to = ((r ^ flip) + ahead) % count
                pairs.append((r * parts + t, to * parts + (t + later) % parts))
        return lax.ppermute(value, ("rx", "tm"), pairs)

    raw = signals.reshape(2, seg_dev * ROWS, HALF)

    cuts = [
        lax.dynamic_slice_in_dim(raw, (me ^ slot) * (segs * ROWS), segs * ROWS, axis=1)
        for slot in range(OFFS)
    ]
    own = [cuts[0]]
    own += [move(cuts[slot], slot) for slot in range(1, OFFS)]
    far = [
        move(own[slot], 0, ahead=OFFS)
        if slot in RELAYED
        else move(cuts[slot], slot, ahead=OFFS)
        for slot in range(OFFS)
    ]

    high, low = halves(forward_table())
    t_high, t_low = halves(inverse_table())

    rows = BLOCKS * segs
    last = OFFS - 1
    spectra = jax.ShapeDtypeStruct((OFFS, rows, 2 * WINDOW), jnp.float32)
    spectrum = jax.ShapeDtypeStruct((1, rows, 2 * WINDOW), jnp.float32)
    sums = jax.ShapeDtypeStruct((OFFS * OFFS * segs, 2 * WINDOW), jnp.float32)
    own_rows = pltpu.VMEM((2 * rows, 2 * BLOCK), jnp.float32)
    far_rows = pltpu.VMEM((rows, 2 * BLOCK), jnp.float32)
    x_own, y_own = pl.pallas_call(
        functools.partial(own_kernel, segs),
        out_shape=(spectra, spectra),
        in_specs=[VMEM] * (last + 2),
        out_specs=(VMEM, VMEM),
        scratch_shapes=[own_rows],
        compiler_params=limit(6),
        name="own",
    )(*own[:last], high, low)
    ready = [
        pl.pallas_call(
            functools.partial(far_kernel, segs),
            out_shape=spectrum,
            in_specs=[VMEM] * 3,
            out_specs=VMEM,
            scratch_shapes=[far_rows],
            compiler_params=limit(4),
            name="far",
        )(piece, high, low)
        for piece in far[: last - 1]
    ]
    x_own, _, total = pl.pallas_call(
        functools.partial(level_kernel, segs),
        out_shape=(spectra, spectra, sums),
        in_specs=[VMEM] * (5 + len(ready)),
        out_specs=(VMEM, VMEM, VMEM),
        scratch_shapes=[own_rows],
        input_output_aliases={3: 0, 4: 1},
        compiler_params=limit(6),
        name="level",
    )(own[last], high, low, x_own, y_own, *ready)
    total = pl.pallas_call(
        functools.partial(ahead_kernel, segs, last - 1),
        out_shape=sums,
        in_specs=[VMEM] * 5,
        out_specs=VMEM,
        scratch_shapes=[pltpu.VMEM(spectrum.shape, jnp.float32), far_rows],
        input_output_aliases={4: 0},
        compiler_params=limit(4),
        name="ahead",
    )(far[last - 1], high, low, x_own, total)

    lag_dev = LAGS // parts
    piece_rows = OFFS * 2 * segs
    sources = []
    for dy in range(2):
        for dt in range(parts):
            slot, part = me ^ (2 * dy), (my_part - dt) % parts
            sources += [(slot, part), (slot ^ 1, part)]
    scale = 1.0 / math.sqrt(2.0 * SEG_LEN * seg_dev * parts)
    d_high, d_low, total = lax.optimization_barrier(
        (*doppler_table(sources, seg_dev, segs, scale), total)
    )
    keep = jax.ShapeDtypeStruct((piece_rows, lag_dev), jnp.float32)
    several = jax.ShapeDtypeStruct((parts, piece_rows, lag_dev), jnp.float32)
    double = jax.ShapeDtypeStruct((2, piece_rows, lag_dev), jnp.float32)
    send, *kept = pl.pallas_call(
        functools.partial(last_kernel, segs, parts),
        out_shape=(several, *(keep,) * parts, *(double,) * parts),
        in_specs=[VMEM] * 7,
        out_specs=(VMEM,) * (1 + 2 * parts),
        scratch_shapes=[
            pltpu.VMEM(spectrum.shape, jnp.float32),
            far_rows,
            pltpu.VMEM(sums.shape, jnp.float32),
            pltpu.VMEM((OFFS * parts, piece_rows, lag_dev), jnp.float32),
        ],
        compiler_params=limit(8),
        name="last",
    )(far[last], high, low, x_own, total, t_high, t_low)
    kept, leaving = kept[:parts], kept[parts:]
    got = move(send, 1)
    crossing = [move(leaving[dt], 2, later=dt) for dt in reversed(range(parts))]
    crossing.reverse()
    straight = [move(jnp.stack([kept[dt], got[dt]]), 0, later=dt) for dt in range(1, parts)]
    turned = pl.pallas_call(
        turn_kernel,
        out_shape=several,
        in_specs=[VMEM] * parts,
        out_specs=VMEM,
        compiler_params=limit(1),
        name="turn",
    )(*crossing)
    crossed = move(turned, 1)
    out_rows = lag_dev * 2 * OFFS * DOPK // HALF
    out = pl.pallas_call(
        functools.partial(doppler_kernel, segs, parts),
        out_shape=jax.ShapeDtypeStruct((out_rows, HALF), jnp.float32),
        in_specs=[VMEM] * (2 * parts + 4),
        out_specs=ANY,
        scratch_shapes=[
            pltpu.VMEM((out_rows, HALF), jnp.float32),
            pltpu.SemaphoreType.DMA((STORES,)),
        ],
        compiler_params=limit(6),
        name="doppler",
    )(kept[0], got, *straight, *crossing, crossed, d_high, d_low)
    return out.reshape(lag_dev, 2, 1, OFFS, 1, DOPK)


def solution(mesh):
    count, parts = mesh.shape["rx"], mesh.shape["tm"]

    def body(signals):
        return per_device(count, parts, signals)

    return jax.shard_map(
        body,
        mesh=mesh,
        in_specs=(P(None, "rx", "tm"),),
        out_specs=P("tm", None, "rx", None, None, None),
        check_vma=False,
    )
```

```python
import functools
import math

import jax
import jax.numpy as jnp
import numpy as np
from jax import lax
from jax.experimental import pallas as pl
from jax.experimental.pallas import tpu as pltpu
from jax.sharding import PartitionSpec as P


SEG_LEN = 4096
LAGS = 256
DOPLEN = 512
DOPK = 256
OFFS = 4

HALF = LAGS // 2
BLOCK = LAGS
WINDOW = 2 * LAGS
BLOCKS = SEG_LEN // BLOCK
ROWS = SEG_LEN // HALF
CLASSES = 4
WIDE = WINDOW // CLASSES * 2
STORES = 4

VMEM = pl.BlockSpec(memory_space=pltpu.VMEM)
ANY = pl.BlockSpec(memory_space=pl.ANY)


def limit(mib):
    return pltpu.CompilerParams(vmem_limit_bytes=mib << 20)


RELAYED = (0, 2, 3)


def halves(table):
    high = table.astype(jnp.bfloat16)
    return jnp.asarray(high), jnp.asarray((table - high.astype(np.float64)).astype(jnp.bfloat16))


def forward_table():
    blocks = []
    for first in range(CLASSES):
        turns = np.outer(np.arange(HALF), np.arange(first, WINDOW, CLASSES)) % WINDOW
        cos, sin = np.cos(2.0 * math.pi / WINDOW * turns), np.sin(2.0 * math.pi / WINDOW * turns)
        blocks.append(np.block([[cos, -sin], [sin, cos]]))
    return np.concatenate(blocks, axis=0)


def inverse_table():
    blocks = []
    for first in range(CLASSES):
        turns = np.outer(np.arange(first, WINDOW, CLASSES), np.arange(HALF)) % WINDOW
        cos, sin = np.cos(2.0 * math.pi / WINDOW * turns), np.sin(2.0 * math.pi / WINDOW * turns)
        blocks.append(np.block([[cos, sin], [-sin, cos]]) / WINDOW)
    return np.concatenate(blocks, axis=0)


def split(value):
    high = value.astype(jnp.bfloat16)
    low = (value - high.astype(jnp.float32)).astype(jnp.bfloat16)
    return high, low


def split_table(value):
    high = lax.reduce_precision(value, exponent_bits=8, mantissa_bits=7)
    return high.astype(jnp.bfloat16), (value - high).astype(jnp.bfloat16)


def product(left, table_high, table_low):
    high, low = split(left)
    count = left.shape[0]
    both = jnp.dot(
        jnp.concatenate([high, low], axis=0), table_high, preferred_element_type=jnp.float32
    )
    rest = jnp.dot(high, table_low, preferred_element_type=jnp.float32)
    return both[:count] + both[count:] + rest


def gather_rows(piece_ref, scratch, row, firsts, segs):
    for plane in range(2):
        for position, first in enumerate(firsts):
            column = pl.ds(plane * BLOCK + position * HALF, HALF)
            for block in range(BLOCKS):
                half = (2 * block + first) % ROWS
                scratch[pl.ds(row + block * segs, segs), column] = piece_ref[
                    plane, pl.ds(half, segs, stride=ROWS), :
                ]


def add_turned(total, value, power):
    (a, b), (c, d) = total, value
    return ((a + c, b + d), (a + d, b - c), (a - c, b - d), (a - d, b + c))[power % 4]


def table_block(table_ref, kind):
    return table_ref[kind * WIDE : (kind + 1) * WIDE, :]


def transform(scratch, table_high, table_low, store, count, whole):
    def part(first, place):
        rows = slice(first, first + count)
        real, imag = place * HALF, BLOCK + place * HALF
        return scratch[rows, real : real + HALF], scratch[rows, imag : imag + HALF]

    odd, even = part(0, 0), part(0, 1)
    for kind in range(CLASSES):
        value = add_turned(odd, even, kind)
        left = jnp.concatenate(value, axis=1)
        if whole:
            value = add_turned(value, part(count, 1), -kind)
            value = add_turned(value, part(count, 0), 2 * kind)
            left = jnp.concatenate([left, jnp.concatenate(value, axis=1)], axis=0)
        out = product(left, table_block(table_high, kind), table_block(table_low, kind))
        store(pl.ds(kind * WIDE, WIDE), out)


def position(parts):
    return lax.rem(lax.axis_index("rx"), OFFS), lax.axis_index("tm") if parts > 1 else 0


def swap_halves(value):
    return pltpu.roll(value, value.shape[0] // 2, axis=0)


def pair_sum(x_ref, x_slot, y_ref, y_slot, column, tile):
    re, im = None, None
    for row in range(0, x_ref.shape[1], tile):
        rows = pl.ds(row, tile)
        x_re = x_ref[x_slot, rows, pl.ds(column, HALF)]
        x_im = x_ref[x_slot, rows, pl.ds(column + HALF, HALF)]
        y_re = y_ref[y_slot, rows, pl.ds(column, HALF)]
        y_im = y_ref[y_slot, rows, pl.ds(column + HALF, HALF)]
        more_re = x_re * y_re + x_im * y_im
        more_im = x_im * y_re - x_re * y_im
        re, im = (more_re, more_im) if re is None else (re + more_re, im + more_im)
    return re, im


def near_pairs(segs, me, x_ref, y_ref, spectrum):
    tile = 2 * segs
    first_half = lax.broadcasted_iota(jnp.int32, (tile, HALF), 0) < segs
    zero = jnp.zeros((tile, HALF), jnp.float32)
    for q in range(OFFS):
        for column in range(0, 2 * WINDOW, WIDE):
            sums = [
                pair_sum(x_ref, q ^ me, y_ref, (q - 1 - o) ^ me, column, tile)
                if o < q
                else (zero, zero)
                for o in range(OFFS)
            ]
            for o in range(0, OFFS, 2):
                rows = pl.ds((q * OFFS + o) * segs, tile)
                for part, base in ((0, 0), (1, HALF)):
                    a, b = sums[o][part], sums[o + 1][part]
                    spectrum[rows, pl.ds(base + column, HALF)] = jnp.where(
                        first_half, a, b
                    ) + swap_halves(jnp.where(first_half, b, a))


def far_pair(segs, q, r, x_ref, x_slot, y_ref, spectrum, first_row):
    tile = 2 * segs
    o = q + (OFFS - 1) - r

    @pl.when(q <= r)
    def _():
        second = lax.broadcasted_iota(jnp.int32, (tile, HALF), 0) >= segs
        mine = second == (lax.rem(o, 2) == 1)
        rows = pl.ds(pl.multiple_of(first_row + (o - lax.rem(o, 2)) * segs, tile), tile)
        for column in range(0, 2 * WINDOW, WIDE):
            sums = pair_sum(x_ref, x_slot, y_ref, 0, column, tile)
            for value, base in zip(sums, (0, HALF)):
                columns = pl.ds(base + column, HALF)
                total = value + swap_halves(value)
                spectrum[rows, columns] = spectrum[rows, columns] + jnp.where(mine, total, 0.0)


def own_transform(piece, slot, table_high, table_low, x_out, y_out, scratch, segs):
    rows = BLOCKS * segs
    gather_rows(piece, scratch, 0, (1, 2), segs)
    gather_rows(piece, scratch, rows, (3, 0), segs)

    def store(columns, value):
        y_out[slot, :, columns] = value[:rows]
        x_out[slot, :, columns] = value[rows:]

    transform(scratch, table_high, table_low, store, rows, True)


def own_kernel(segs, *refs):
    pieces, (table_high, table_low, x_out, y_out, scratch) = refs[:-5], refs[-5:]
    for slot, piece in enumerate(pieces):
        own_transform(piece, slot, table_high, table_low, x_out, y_out, scratch, segs)


def far_transform(piece, table_high, table_low, y_out, scratch, segs):
    gather_rows(piece, scratch, 0, (1, 2), segs)

    def store(columns, value):
        y_out[0, :, columns] = value

    transform(scratch, table_high, table_low, store, BLOCKS * segs, False)


def far_kernel(segs, piece, table_high, table_low, y_out, scratch):
    far_transform(piece, table_high, table_low, y_out, scratch, segs)


def level_kernel(segs, piece, table_high, table_low, x_in, y_in, *refs):
    del x_in, y_in
    ready, (x_out, y_out, spectrum, scratch) = refs[:-4], refs[-4:]
    me, _ = position(1)
    own_transform(piece, OFFS - 1, table_high, table_low, x_out, y_out, scratch, segs)
    near_pairs(segs, me, x_out, y_out, spectrum)
    for slot, y_ref in enumerate(ready):
        for x_slot in range(OFFS):
            q = me ^ x_slot
            far_pair(segs, q, me ^ slot, x_out, x_slot, y_ref, spectrum, q * (OFFS * segs))


def ahead_kernel(
    segs, slot, piece, table_high, table_low, x_ref, _, spectrum, y_scratch, scratch
):
    far_transform(piece, table_high, table_low, y_scratch, scratch, segs)
    me, _ = position(1)
    for x_slot in range(OFFS):
        q = me ^ x_slot
        far_pair(segs, q, me ^ slot, x_ref, x_slot, y_scratch, spectrum, q * (OFFS * segs))


def last_kernel(segs, parts, piece, table_high, table_low, x_ref, sums, t_high, t_low, *refs):
    outs, (y_ref, scratch, spectrum, held) = refs[:-4], refs[-4:]
    far_transform(piece, table_high, table_low, y_ref, scratch, segs)
    me, my_part = position(parts)
    tile = 2 * segs
    lag_dev = LAGS // parts
    count = OFFS * segs
    for x_slot in range(OFFS):
        q = me ^ x_slot
        spectrum[pl.ds(x_slot * count, count), :] = sums[
            pl.ds(pl.multiple_of(q * count, count), count), :
        ]
        far_pair(segs, q, me ^ (OFFS - 1), x_ref, x_slot, y_ref, spectrum, x_slot * count)
    early, late = None, None
    for kind in range(CLASSES):
        out = product(
            spectrum[:, kind * WIDE : (kind + 1) * WIDE],
            table_block(t_high, kind),
            table_block(t_low, kind),
        )
        value = (out[:, :HALF], out[:, HALF:])
        early = add_turned(early, value, kind) if early else value
        late = add_turned(late, value, 0) if late else value
    corr_re = jnp.concatenate([early[0], late[0]], axis=1)
    corr_im = jnp.concatenate([early[1], late[1]], axis=1)
    wide_half = lax.broadcasted_iota(jnp.int32, (tile, LAGS), 0) < segs
    for index in range(OFFS):
        for o in range(0, OFFS, 2):
            row = (index * OFFS + o) * segs
            re, im = corr_re[row : row + tile], corr_im[row : row + tile]
            first = jnp.where(wide_half, re, swap_halves(im))
            second = jnp.where(wide_half, swap_halves(re), im)
            for t in range(parts):
                lanes = slice(t * lag_dev, (t + 1) * lag_dev)
                held[index * parts + t, pl.ds(o * tile, tile), :] = first[:, lanes]
                held[index * parts + t, pl.ds((o + 1) * tile, tile), :] = second[:, lanes]
    send, keeps, crossing = outs[0], outs[1 : 1 + parts], outs[1 + parts :]
    for dt in range(parts):
        there = lax.rem(my_part + dt, parts)
        keeps[dt][...] = held[there]
        send[dt] = held[parts + there]
        crossing[dt][0] = held[2 * parts + there]
        crossing[dt][1] = held[3 * parts + there]


def turn_kernel(*refs):
    for index, piece in enumerate(refs[:-1]):
        refs[-1][index] = piece[1]


def doppler_kernel(segs, parts, keep_ref, recv_ref, *refs):
    straight, crossing = refs[: parts - 1], refs[parts - 1 : 2 * parts - 1]
    cross_ref, table_high, table_low, out_ref, scratch, sems = refs[2 * parts - 1 :]
    tile = 2 * segs
    lag_dev = keep_ref.shape[1]
    stride = scratch.shape[0] // lag_dev
    per = DOPK // HALF
    table = jnp.concatenate([table_high[...], table_high[...], table_low[...]], axis=0)
    outs = []
    for o in range(OFFS):
        rows = pl.ds(o * tile, tile)
        tiles = [keep_ref[rows, :], recv_ref[0, rows, :]]
        for other in straight:
            tiles += [other[0, rows, :], other[1, rows, :]]
        for dt, other in enumerate(crossing):
            tiles += [other[0, rows, :], cross_ref[dt, rows, :]]
        high, low = split(jnp.concatenate(tiles, axis=0))
        left = jnp.concatenate([high, low, high], axis=0)
        outs.append(
            lax.dot_general(
                left, table, (((0,), (0,)), ((), ())), preferred_element_type=jnp.float32
            )
        )
    lags = lag_dev // STORES
    copies = []
    for store in range(STORES):
        base = store * lags
        span = pl.ds(base * stride, lags * stride)
        planes = [
            outs[o][base : base + lags, c * DOPK + f * HALF : c * DOPK + (f + 1) * HALF]
            for c in range(2)
            for o in range(OFFS)
            for f in range(per)
        ]
        scratch[span, :] = jnp.swapaxes(jnp.stack(planes), 0, 1).reshape(lags * stride, HALF)
        copies.append(pltpu.make_async_copy(scratch.at[span], out_ref.at[span], sems.at[store]))
        copies[-1].start(priority=store % 2)
    for copy in copies:
        copy.wait()


def doppler_table(sources, seg_dev, segs, scale):
    segment = jnp.concatenate(
        [part * seg_dev + slot * segs + jnp.arange(segs, dtype=jnp.int32) for slot, part in sources]
    )
    frequency = jnp.arange(DOPK, dtype=jnp.int32) - DOPK // 2
    angle = (
        2.0 * math.pi / DOPLEN
        * (segment[:, None] * frequency[None, :] % DOPLEN).astype(jnp.float32)
    )
    cos, sin = (jnp.cos(angle) * scale, jnp.sin(angle) * scale)
    cos = cos.reshape(len(sources), 1, segs, DOPK)
    sin = sin.reshape(len(sources), 1, segs, DOPK)
    table = jnp.concatenate(
        [jnp.concatenate([cos, -sin], axis=3), jnp.concatenate([sin, cos], axis=3)], axis=1
    ).reshape(2 * len(sources) * segs, 2 * DOPK)
    return split_table(table)


def per_device(count, parts, signals):
    rec_dev, length = signals.shape[1], signals.shape[2]
    seg_dev = length // SEG_LEN
    segs = seg_dev // OFFS
    assert rec_dev == 1 and count % OFFS == 0 and seg_dev % OFFS == 0
    me = lax.axis_index("rx") % OFFS
    my_part = lax.axis_index("tm")

    def move(value, flip, ahead=0, later=0):
        pairs = []
        for r in range(count):
            for t in range(parts):
                to = ((r ^ flip) + ahead) % count
                pairs.append((r * parts + t, to * parts + (t + later) % parts))
        return lax.ppermute(value, ("rx", "tm"), pairs)

    raw = signals.reshape(2, seg_dev * ROWS, HALF)

    cuts = [
        lax.dynamic_slice_in_dim(raw, (me ^ slot) * (segs * ROWS), segs * ROWS, axis=1)
        for slot in range(OFFS)
    ]
    own = [cuts[0]]
    own += [move(cuts[slot], slot) for slot in range(1, OFFS)]
    far = [
        move(own[slot], 0, ahead=OFFS)
        if slot in RELAYED
        else move(cuts[slot], slot, ahead=OFFS)
        for slot in range(OFFS)
    ]

    high, low = halves(forward_table())
    t_high, t_low = halves(inverse_table())

    rows = BLOCKS * segs
    last = OFFS - 1
    spectra = jax.ShapeDtypeStruct((OFFS, rows, 2 * WINDOW), jnp.float32)
    spectrum = jax.ShapeDtypeStruct((1, rows, 2 * WINDOW), jnp.float32)
    sums = jax.ShapeDtypeStruct((OFFS * OFFS * segs, 2 * WINDOW), jnp.float32)
    own_rows = pltpu.VMEM((2 * rows, 2 * BLOCK), jnp.float32)
    far_rows = pltpu.VMEM((rows, 2 * BLOCK), jnp.float32)
    x_own, y_own = pl.pallas_call(
        functools.partial(own_kernel, segs),
        out_shape=(spectra, spectra),
        in_specs=[VMEM] * (last + 2),
        out_specs=(VMEM, VMEM),
        scratch_shapes=[own_rows],
        compiler_params=limit(6),
        name="own",
    )(*own[:last], high, low)
    ready = [
        pl.pallas_call(
            functools.partial(far_kernel, segs),
            out_shape=spectrum,
            in_specs=[VMEM] * 3,
            out_specs=VMEM,
            scratch_shapes=[far_rows],
            compiler_params=limit(4),
            name="far",
        )(piece, high, low)
        for piece in far[: last - 1]
    ]
    x_own, _, total = pl.pallas_call(
        functools.partial(level_kernel, segs),
        out_shape=(spectra, spectra, sums),
        in_specs=[VMEM] * (5 + len(ready)),
        out_specs=(VMEM, VMEM, VMEM),
        scratch_shapes=[own_rows],
        input_output_aliases={3: 0, 4: 1},
        compiler_params=limit(6),
        name="level",
    )(own[last], high, low, x_own, y_own, *ready)
    total = pl.pallas_call(
        functools.partial(ahead_kernel, segs, last - 1),
        out_shape=sums,
        in_specs=[VMEM] * 5,
        out_specs=VMEM,
        scratch_shapes=[pltpu.VMEM(spectrum.shape, jnp.float32), far_rows],
        input_output_aliases={4: 0},
        compiler_params=limit(4),
        name="ahead",
    )(far[last - 1], high, low, x_own, total)

    lag_dev = LAGS // parts
    piece_rows = OFFS * 2 * segs
    sources = []
    for dy in range(2):
        for dt in range(parts):
            slot, part = me ^ (2 * dy), (my_part - dt) % parts
            sources += [(slot, part), (slot ^ 1, part)]
    scale = 1.0 / math.sqrt(2.0 * SEG_LEN * seg_dev * parts)
    d_high, d_low, total = lax.optimization_barrier(
        (*doppler_table(sources, seg_dev, segs, scale), total)
    )
    keep = jax.ShapeDtypeStruct((piece_rows, lag_dev), jnp.float32)
    several = jax.ShapeDtypeStruct((parts, piece_rows, lag_dev), jnp.float32)
    double = jax.ShapeDtypeStruct((2, piece_rows, lag_dev), jnp.float32)
    send, *kept = pl.pallas_call(
        functools.partial(last_kernel, segs, parts),
        out_shape=(several, *(keep,) * parts, *(double,) * parts),
        in_specs=[VMEM] * 7,
        out_specs=(VMEM,) * (1 + 2 * parts),
        scratch_shapes=[
            pltpu.VMEM(spectrum.shape, jnp.float32),
            far_rows,
            pltpu.VMEM(sums.shape, jnp.float32),
            pltpu.VMEM((OFFS * parts, piece_rows, lag_dev), jnp.float32),
        ],
        compiler_params=limit(8),
        name="last",
    )(far[last], high, low, x_own, total, t_high, t_low)
    kept, leaving = kept[:parts], kept[parts:]
    got = move(send, 1)
    crossing = [move(leaving[dt], 2, later=dt) for dt in reversed(range(parts))]
    crossing.reverse()
    straight = [move(jnp.stack([kept[dt], got[dt]]), 0, later=dt) for dt in range(1, parts)]
    turned = pl.pallas_call(
        turn_kernel,
        out_shape=several,
        in_specs=[VMEM] * parts,
        out_specs=VMEM,
        compiler_params=limit(1),
        name="turn",
    )(*crossing)
    crossed = move(turned, 1)
    out_rows = lag_dev * 2 * OFFS * DOPK // HALF
    out = pl.pallas_call(
        functools.partial(doppler_kernel, segs, parts),
        out_shape=jax.ShapeDtypeStruct((out_rows, HALF), jnp.float32),
        in_specs=[VMEM] * (2 * parts + 4),
        out_specs=ANY,
        scratch_shapes=[
            pltpu.VMEM((out_rows, HALF), jnp.float32),
            pltpu.SemaphoreType.DMA((STORES,)),
        ],
        compiler_params=limit(6),
        name="doppler",
    )(kept[0], got, *straight, *crossing, crossed, d_high, d_low)
    return out.reshape(lag_dev, 2, 1, OFFS, 1, DOPK)


def solution(mesh):
    count, parts = mesh.shape["rx"], mesh.shape["tm"]

    def body(signals):
        return per_device(count, parts, signals)

    return jax.shard_map(
        body,
        mesh=mesh,
        in_specs=(P(None, "rx", "tm"),),
        out_specs=P("tm", None, "rx", None, None, None),
        check_vma=False,
    )
```
